256 devices in a mesh: grp: 16 (over y, x), leaf: 16 (over z, core).
Axes of the slice: x: 4, y: 4, z: 8, core: 2. Of those that a mesh axis runs over, the one named last changes fastest.
Arguments:
- direction: bfloat16 [393216, 256], P(('grp', 'leaf')), may hold values from -6 to 6
- residual: bfloat16 [393216, 256], P(('grp', 'leaf')), may hold values from -6 to 6
- leaf_order: int32 [256, 1536], P(('grp', 'leaf')), may hold values from 0 to 1535, as said below
- diag_block: bfloat16 [256, 1536, 1536], P(('grp', 'leaf')), may hold values from -0.15625 to 0.15625
- up_basis: bfloat16 [256, 1536, 128], P(('grp', 'leaf')), may hold values from -0.15625 to 0.15625
- down_basis: bfloat16 [256, 1536, 128], P(('grp', 'leaf')), may hold values from -0.5 to 0.5
- leaf_ops: bfloat16 [3, 256, 128, 128], P(None, ('grp', 'leaf')), may hold values from -0.375 to 0.375
- inner_ops: bfloat16 [3, 224, 128, 128], P(None, 'grp'), may hold values from -0.375 to 0.375
- top_ops: bfloat16 [3, 30, 128, 128], replicated, may hold values from -0.375 to 0.375
- ridge_shift: float32 [1], replicated, may hold values from 0.5 to 2
Outputs:
- image: bfloat16 [393216, 256], P(('grp', 'leaf'))
- curvature_gram: float32 [256, 256], replicated
- residual_gram: float32 [256, 256], replicated
The draws below stay inside these ranges and needn't reach their ends.
Inputs may be any that keep to these rules, and one draw needn't show every extreme that they name: Each row of leaf_order is a permutation of 0 to 1535.
All inputs are finite; a program needn't handle non-finite values.
Results may differ from the reference program's by a relative error of at most 0.022.
Values may be sent and summed in bfloat16 or wider, within the bound.
A program may use at most 64 MiB of HBM per device.

```python
import math
import jax
import jax.numpy as jnp
from jax import lax

LEAF = 1536
RANK = 128
NRHS = 256
LEAVES = 256
POINTS = 393216
INNER = 224
UPPER = 30
N_GRP = 16
N_LEAF = 16


def draw_leaf_order(key, part):
    row_keys = jax.random.split(jax.random.fold_in(key, 17), LEAVES)
    return jax.vmap(lambda single: jax.random.permutation(single, LEAF))(row_keys).astype(jnp.int32)


def block_levels(stream_key, shape, shards, low, top_value):
    loudness, own = 1.0, jax.random.fold_in(stream_key, 6)
    for position, shards_of in shards:
        steps = jnp.exp(jax.random.uniform(jax.random.fold_in(own, position), (shards_of,), jnp.float32, low / len(shards), top_value / len(shards)))
        loudness = loudness * jnp.repeat(steps, shape[position] // shards_of).reshape([-1 if axis == position else 1 for axis in range(len(shape))])
    return loudness


def centred(own_key, dims, scale, bound, cuts=(), kind=jnp.bfloat16):
    gain = block_levels(own_key, dims, cuts, -0.22, 0.18) if cuts else 1.0
    drawn = jax.random.normal(own_key, dims, jnp.float32) * scale * gain
    return jnp.minimum(jnp.maximum(drawn, -bound), bound).astype(kind)


def setup_inputs(seed: int = 0) -> dict:
    keys = jax.random.split(jax.random.key(seed), 11)
    direction = centred(keys[0], (POINTS, NRHS), 1.0, 6.0, ((0, 256),))
    residual = centred(keys[1], (POINTS, NRHS), 1.0, 6.0, ((0, 256),))
    leaf_order = draw_leaf_order(jax.random.fold_in(keys[10], 71), 0)
    diag_block = centred(keys[3], (LEAVES, LEAF, LEAF), LEAF ** -0.5, 0.15625, ((0, 256),))
    up_basis = centred(keys[4], (LEAVES, LEAF, RANK), LEAF ** -0.5, 0.15625, ((0, 256),))
    down_basis = centred(keys[5], (LEAVES, LEAF, RANK), RANK ** -0.5, 0.5, ((0, 256),))
    leaf_ops = centred(keys[6], (3, LEAVES, RANK, RANK), (2 * RANK) ** -0.5, 0.375, ((1, 256),))
    inner_ops = centred(keys[7], (3, INNER, RANK, RANK), (2 * RANK) ** -0.5, 0.375, ((1, 16),))
    top_ops = centred(keys[8], (3, UPPER, RANK, RANK), (2 * RANK) ** -0.5, 0.375)
    ridge_shift = jnp.clip(jnp.exp(jax.random.uniform(keys[9], (1,), jnp.float32, math.log(0.5), math.log(2.0))), 0.5, 2.0)
    return {"direction": direction, "residual": residual, "leaf_order": leaf_order, "diag_block": diag_block, "up_basis": up_basis, "down_basis": down_basis, "leaf_ops": leaf_ops, "inner_ops": inner_ops, "top_ops": top_ops, "ridge_shift": ridge_shift}


def level_operators(height, leaf_ops, inner_ops, top_ops):
    leaf_levels = N_LEAF.bit_length() - 1
    if height == 0:
        return leaf_ops
    if height < leaf_levels:
        offset = sum(N_LEAF >> section for section in range(1, height))
        node_count = N_LEAF >> height
        grouped = inner_ops.reshape(3, N_GRP, N_LEAF - 2, RANK, RANK)
        return grouped[:, :, offset:offset + node_count].reshape(3, N_GRP * node_count, RANK, RANK)
    upper_level = height - leaf_levels
    offset = sum(N_GRP >> section for section in range(upper_level))
    return top_ops[:, offset:offset + (N_GRP >> upper_level)]


def contribute(transfer, skeletons):
    product = jnp.einsum("nrs,nrk->nsk", transfer.astype(jnp.float32), skeletons.astype(jnp.float32))
    return product.astype(jnp.bfloat16)


def pair_sum(lifted):
    shaped = lifted.astype(jnp.float32).reshape(-1, 2, lifted.shape[1], lifted.shape[2])
    return (shaped[:, 0] + shaped[:, 1]).astype(jnp.bfloat16)


def project_up(pieces):
    return jnp.dot(pieces[0].T, pieces[1], preferred_element_type=jnp.float32).astype(jnp.bfloat16)


def leaf_apply(pieces):
    dense = jnp.dot(pieces[0], pieces[1], preferred_element_type=jnp.float32)
    return dense + jnp.dot(pieces[2], pieces[3], preferred_element_type=jnp.float32)


def reference(direction, residual, leaf_order, diag_block, up_basis, down_basis, leaf_ops, inner_ops, top_ops, ridge_shift):
    total_levels = (N_LEAF.bit_length() - 1) + (N_GRP.bit_length() - 1)
    blocks = direction.reshape(LEAVES, LEAF, NRHS)
    ordered = jnp.take_along_axis(blocks, leaf_order[:, :, None], axis=1)
    skeleton = lax.map(project_up, (up_basis, ordered))
    level_skeletons = [skeleton]
    for height in range(total_levels):
        operators = level_operators(height, leaf_ops, inner_ops, top_ops)
        skeleton = pair_sum(contribute(operators[0], skeleton))
        level_skeletons.append(skeleton)
    coarse = jnp.zeros((1, RANK, NRHS), jnp.bfloat16)
    for height in reversed(range(total_levels)):
        operators = level_operators(height, leaf_ops, inner_ops, top_ops)
        below = level_skeletons[height]
        sibling = jnp.flip(below.reshape(-1, 2, RANK, NRHS), axis=1).reshape(below.shape)
        parent = jnp.repeat(coarse, 2, axis=0)
        coupled = jnp.einsum("nrs,nsk->nrk", operators[2].astype(jnp.float32), sibling.astype(jnp.float32))
        passed = jnp.einsum("nrs,nsk->nrk", operators[1].astype(jnp.float32), parent.astype(jnp.float32))
        coarse = (coupled + passed).astype(jnp.bfloat16)
    local = lax.map(leaf_apply, (diag_block, ordered, down_basis, coarse))
    row_index = jnp.arange(LEAVES, dtype=jnp.int32)[:, None]
    restored = jnp.zeros_like(local).at[row_index, leaf_order].set(local)
    image = (restored.reshape(POINTS, NRHS) + ridge_shift[0] * direction.astype(jnp.float32)).astype(jnp.bfloat16)
    curvature = jnp.dot(direction.T, image, preferred_element_type=jnp.float32) / POINTS
    correlation = jnp.dot(residual.T, image, preferred_element_type=jnp.float32) / POINTS
    return (image, curvature, correlation)
```

```python
import jax
import jax.numpy as jnp
from jax import lax
from jax.experimental import pallas as pl
from jax.experimental.pallas import tpu as pltpu
from jax.sharding import PartitionSpec as P

F32 = jnp.float32
BF16 = jnp.bfloat16
GRP_LEAF = ("grp", "leaf")
N = 1536
R = 128
K = 256
D = 16
C = K // D


def mm(a, b):
    return lax.dot_general(a, b, (((1,), (0,)), ((), ())), preferred_element_type=F32)


def mmt(a, b):
    return lax.dot_general(a, b, (((1,), (1,)), ((), ())), preferred_element_type=F32)


def kernel(
    x_h, res_h, ord_h, diag_h, up_h, dn_h, lop_h, iop_h, top_h, ridge_s,
    img_h, cur_h, cor_h,
    x_v, res_v, ord_v, diag_v, up_v, dn_v, lop_v, iop_v, top_v,
    p_v, pt_v, og_v, xt_v, loc_v, im_v, img_v,
    s0_v, sib_v, l1_v, a_r, root_v, b_r, t_v, q_v, vr_v, c_v, c_r,
    gs_v, gs_r, own_v, h_v, h_r, z_v, z_r, f_v, f_r, o_r, out_v,
    load_sem, pair_s, pair_r, a_ss, a_rs, b_ss, b_rs, c_ss, c_rs,
    h_ss, h_rs, z_ss, z_rs, f_ss, f_rs, o_ss, o_rs, store_sem,
):
    me = lax.axis_index("leaf")
    g = lax.axis_index("grp")
    core = lax.rem(me, 2)
    z = me // 2
    sibling = me + 1 - 2 * core

    def other(base, r):
        return lax.rem(base + r, D)

    def sib_of(a):
        return a + 1 - 2 * lax.rem(a, 2)

    def to_leaf(src, dst, ss, rs, j):
        return pltpu.make_async_remote_copy(
            src_ref=src, dst_ref=dst, send_sem=ss, recv_sem=rs,
            device_id={"leaf": j}, device_id_type=pl.DeviceIdType.MESH)

    def to_grp(src, dst, ss, rs, j):
        return pltpu.make_async_remote_copy(
            src_ref=src, dst_ref=dst, send_sem=ss, recv_sem=rs,
            device_id={"grp": j}, device_id_type=pl.DeviceIdType.MESH)

    loads = [
        pltpu.make_async_copy(src, dst, load_sem.at[i])
        for i, (src, dst) in enumerate([
            (ord_h, ord_v), (up_h.at[0], up_v), (lop_h.at[:, 0], lop_v), (x_h, x_v),
            (iop_h, iop_v), (top_h, top_v), (diag_h.at[0], diag_v), (res_h, res_v), (dn_h.at[0], dn_v)])
    ]
    for copy in loads:
        copy.start()
    l_ord, l_up, l_lop, l_x, l_iop, l_top, l_diag, l_res, l_dn = loads

    barrier = pltpu.get_barrier_semaphore()
    for r in range(1, D):
        pl.semaphore_signal(barrier, inc=1, device_id={"leaf": other(me, r)}, device_id_type=pl.DeviceIdType.MESH)
        pl.semaphore_signal(barrier, inc=1, device_id={"grp": other(g, r)}, device_id_type=pl.DeviceIdType.MESH)

    l_ord.wait()
    order = ord_v[...]
    column = jnp.broadcast_to(order.astype(F32), (R, N)).T.astype(jnp.int32)
    lane = lax.broadcasted_iota(jnp.int32, (N, R), 1)
    low = jnp.where((column & (R - 1)) == lane, 1.0, 0.0).astype(BF16)
    high = (column >> 7).astype(BF16)
    for j in range(N // R):
        p_v[:, j * R:(j + 1) * R] = jnp.where(high == jnp.asarray(j, BF16), low, jnp.zeros_like(low))

    l_up.wait()
    l_lop.wait()
    up_t = up_v[...].T
    lift_t = lax.dot_general(lop_v[0], up_t, (((0,), (0,)), ((), ())), preferred_element_type=F32).astype(BF16)
    both_t = jnp.concatenate([up_t, lift_t], axis=0)

    l_x.wait()
    for t in range(3):
        rows = pl.ds(t * 512, 512)
        og_v[rows, :] = mm(p_v[rows, :], x_v[...]).astype(BF16)
    both = mm(both_t, og_v[...]).T
    s0_v[...] = both[:, :R].astype(BF16)
    l1_v[...] = both[:, R:].astype(BF16).reshape(D, C, R)

    pl.semaphore_wait(barrier, 2 * (D - 1))

    sends_a = []
    for r in range(1, D):
        j = other(me, r)
        copy = to_leaf(l1_v.at[j], a_r.at[me], a_ss.at[r], a_rs.at[me], j)
        copy.start()
        sends_a.append(copy)
    pair = to_leaf(s0_v, sib_v, pair_s.at[0], pair_r.at[0], sibling)
    pair.start()
    a_r[me] = l1_v[me]

    l_iop.wait()
    l_top.wait()
    up2 = [mm(iop_v[0, 8 + 2 * m:10 + 2 * m].reshape(2 * R, R), iop_v[0, 12 + m]).astype(BF16) for m in range(2)]
    up1 = [mm(iop_v[0, 2 * m:2 * m + 2].reshape(2 * R, R), up2[m // 2][(m % 2) * R:(m % 2 + 1) * R]).astype(BF16)
           for m in range(4)]

    for r in range(1, D):
        j = other(me, r)
        to_leaf(l1_v.at[j], a_r.at[j], a_ss.at[r], a_rs.at[j], j).wait_recv()
    s1 = [(a_r[2 * m].astype(F32) + a_r[2 * m + 1].astype(F32)).astype(BF16) for m in range(8)]
    s1p = [jnp.concatenate(s1[2 * m:2 * m + 2], axis=1) for m in range(4)]
    root = mm(s1p[0], up1[0])
    for m in range(1, 4):
        root = root + mm(s1p[m], up1[m])
    root_v[...] = root.astype(BF16)

    sends_b = []
    for r in range(1, D):
        j = other(g, r)
        copy = to_grp(root_v, b_r.at[g], b_ss.at[r], b_rs.at[g], j)
        copy.start()
        sends_b.append(copy)
    b_r[g] = root_v[...]

    s2 = [mm(s1p[m], iop_v[0, 2 * m:2 * m + 2].reshape(2 * R, R)).astype(BF16) for m in range(4)]
    s2p = [jnp.concatenate(s2[2 * m:2 * m + 2], axis=1) for m in range(2)]
    s3 = [mm(s2p[m], iop_v[0, 8 + 2 * m:10 + 2 * m].reshape(2 * R, R)).astype(BF16) for m in range(2)]
    c3 = [mmt(s3[1 - m], iop_v[2, 12 + m]).astype(BF16) for m in range(2)]
    c2 = [(mmt(s2[m ^ 1], iop_v[2, 8 + m]) + mmt(c3[m // 2], iop_v[1, 8 + m])).astype(BF16) for m in range(4)]
    c1 = [mmt(s1[m ^ 1], iop_v[2, m]) + mmt(c2[m // 2], iop_v[1, m]) for m in range(8)]
    q2 = [mm(iop_v[1, 8 + m], iop_v[1, 12 + m // 2]).astype(BF16) for m in range(4)]
    for m in range(8):
        q_v[m] = mm(iop_v[1, m], q2[m // 2]).astype(BF16)

    a4, a5, a6, a7 = g, g // 2, g // 4, g // 8
    y5 = top_v[1, a4]
    y6 = mm(y5, top_v[1, 16 + a5]).astype(BF16)
    y7 = mm(y6, top_v[1, 24 + a6]).astype(BF16)
    x5 = mm(y5, top_v[2, 16 + a5]).astype(BF16)
    x6 = mm(y6, top_v[2, 24 + a6]).astype(BF16)
    x7 = mm(y7, top_v[2, 28 + a7]).astype(BF16)

    def lifts(base, node, count):
        return top_v[0, pl.ds(base + node, count)].reshape(count * R, R)

    t_v[g] = jnp.zeros((R, R), BF16)
    n4, n5, n6, n7 = sib_of(a4), sib_of(a5), sib_of(a6), sib_of(a7)
    t_v[n4] = top_v[2, a4].T
    t_v[pl.ds(2 * n5, 2)] = mmt(lifts(0, 2 * n5, 2), x5).astype(BF16).reshape(2, R, R)
    w = mmt(lifts(16, 2 * n6, 2), x6).astype(BF16)
    for b in range(2):
        t_v[pl.ds(4 * n6 + 2 * b, 2)] = mm(lifts(0, 4 * n6 + 2 * b, 2), w[b * R:(b + 1) * R]).astype(BF16).reshape(2, R, R)
    w = mmt(lifts(24, 2 * n7, 2), x7).astype(BF16)
    for b in range(2):
        u = mm(lifts(16, 4 * n7 + 2 * b, 2), w[b * R:(b + 1) * R]).astype(BF16)
        for d in range(2):
            first = 8 * n7 + 4 * b + 2 * d
            t_v[pl.ds(first, 2)] = mm(lifts(0, first, 2), u[d * R:(d + 1) * R]).astype(BF16).reshape(2, R, R)

    for r in range(1, D):
        j = other(g, r)
        to_grp(root_v, b_r.at[j], b_ss.at[r], b_rs.at[j], j).wait_recv()
    c4 = jnp.zeros((C, R), F32)
    for m in range(D // 2):
        c4 = c4 + mm(jnp.concatenate([b_r[2 * m], b_r[2 * m + 1]], axis=1), t_v[2 * m:2 * m + 2].reshape(2 * R, R))
    c4 = c4.astype(BF16)
    for m in range(8):
        c_v[m] = (c1[m] + mmt(c4, q_v[m])).astype(BF16)

    sends_c = []
    for r in range(1, D):
        j = other(me, r)
        copy = to_leaf(c_v.at[j // 2], c_r.at[me], c_ss.at[r], c_rs.at[me], j)
        copy.start()
        sends_c.append(copy)
    c_r[me] = c_v[z]

    l_diag.wait()
    ridge = ridge_s[0]
    for t in range(3):
        rows = pl.ds(t * 512, 512)
        loc_v[rows, :] = mm(diag_v[rows, :], og_v[...]) + ridge * og_v[rows, :].astype(F32)
    l_res.wait()
    xt_v[:K, :] = og_v[...].T
    for t in range(3):
        rows = pl.ds(t * 512, 512)
        xt_v[K:, rows] = mm(p_v[rows, :], res_v[...]).astype(BF16).T
    l_dn.wait()
    vr_v[...] = mm(dn_v[...], lop_v[1]).astype(BF16)
    pair.wait_recv()
    near = mmt(sib_v[...], lop_v[2]).astype(BF16)
    loc_v[...] = loc_v[...] + mmt(dn_v[...], near)
    row = order
    row_low = jnp.broadcast_to(row & (R - 1), (R, N))
    row_high = jnp.broadcast_to(row >> 7, (R, N)).astype(F32).astype(BF16)
    row_one = jnp.where(row_low == lax.broadcasted_iota(jnp.int32, (R, N), 0), 1.0, 0.0).astype(BF16)
    for j in range(N // R):
        pt_v[j * R:(j + 1) * R, :] = jnp.where(row_high == jnp.asarray(j, BF16), row_one, jnp.zeros_like(row_one))

    for r in range(1, D):
        j = other(me, r)
        to_leaf(c_v.at[j // 2], c_r.at[j], c_ss.at[r], c_rs.at[j], j).wait_recv()
    im_v[...] = (loc_v[...] + mmt(vr_v[...], c_r[...].reshape(K, R))).astype(BF16)

    gs_v[...] = mm(xt_v[pl.ds((1 - core) * K, K), :], im_v[...]).astype(BF16)
    swap = to_leaf(gs_v, gs_r, pair_s.at[1], pair_r.at[1], sibling)
    swap.start()
    own_v[...] = mm(xt_v[pl.ds(core * K, K), :], im_v[...])
    swap.wait_recv()
    h_v[...] = (own_v[...] + gs_r[...].astype(F32)).astype(BF16).reshape(D, C, K)
    sends_h = []
    for r in range(1, D):
        j = other(g, r)
        copy = to_grp(h_v.at[j], h_r.at[g], h_ss.at[r], h_rs.at[g], j)
        copy.start()
        sends_h.append(copy)
    h_r[g] = h_v[g]

    stores = []
    for t in range(3):
        rows = pl.ds(t * 512, 512)
        img_v[rows, :] = mm(pt_v[rows, :], im_v[...]).astype(BF16)
        copy = pltpu.make_async_copy(img_v.at[rows], img_h.at[rows], store_sem.at[t])
        copy.start()
        stores.append(copy)

    for r in range(1, D):
        j = other(g, r)
        to_grp(h_v.at[j], h_r.at[j], h_ss.at[r], h_rs.at[j], j).wait_recv()
    total = h_r[0].astype(F32)
    for j in range(1, D):
        total = total + h_r[j].astype(F32)
    z_v[...] = total.astype(BF16)
    sends_z = []
    for r in range(1, D // 2):
        j = lax.rem(me + 2 * r, D)
        copy = to_leaf(z_v, z_r.at[z], z_ss.at[r], z_rs.at[z], j)
        copy.start()
        sends_z.append(copy)
    z_r[z] = z_v[...]
    for r in range(1, D // 2):
        j = lax.rem(me + 2 * r, D)
        to_leaf(z_v, z_r.at[j // 2], z_ss.at[r], z_rs.at[j // 2], j).wait_recv()
    total = z_r[0].astype(F32)
    for j in range(1, D // 2):
        total = total + z_r[j].astype(F32)
    f_v[...] = total.astype(BF16)
    sends_f = []
    for r in range(1, D):
        j = other(g, r)
        copy = to_grp(f_v, f_r.at[g], f_ss.at[r], f_rs.at[g], j)
        copy.start()
        sends_f.append(copy)
    f_r[g] = f_v[...]
    for r in range(D):
        j = other(g, r)
        if r:
            to_grp(f_v, f_r.at[j], f_ss.at[r], f_rs.at[j], j).wait_recv()
        copy = to_leaf(f_r.at[j], o_r.at[j], o_ss.at[j], o_rs.at[j], sibling)
        copy.start()
        sends_f.append(copy)
    scale = 1.0 / (N * D * D)
    out_v[core] = f_r[...].reshape(K, K).astype(F32) * scale
    for j in range(D):
        to_leaf(f_r.at[j], o_r.at[j], o_ss.at[j], o_rs.at[j], sibling).wait_recv()
    out_v[1 - core] = o_r[...].reshape(K, K).astype(F32) * scale
    for i, dst in enumerate((cur_h, cor_h)):
        copy = pltpu.make_async_copy(out_v.at[i], dst, store_sem.at[3 + i])
        copy.start()
        stores.append(copy)

    for copy in [pair, swap, *sends_a, *sends_b, *sends_c, *sends_h, *sends_z, *sends_f]:
        copy.wait_send()
    for copy in stores:
        copy.wait()


def body(*args):
    any_spec = pl.BlockSpec(memory_space=pl.ANY)
    dma = pltpu.SemaphoreType.DMA
    v = pltpu.VMEM
    scratch = [
        v((N, K), BF16), v((N, K), BF16), v((1, N), jnp.int32), v((N, N), BF16), v((N, R), BF16), v((N, R), BF16),
        v((3, R, R), BF16), v((3, 14, R, R), BF16), v((3, 30, R, R), BF16),
        v((N, N), BF16), v((N, N), BF16), v((N, K), BF16), v((2 * K, N), BF16), v((N, K), F32), v((N, K), BF16), v((N, K), BF16),
        v((K, R), BF16), v((K, R), BF16), v((D, C, R), BF16), v((D, C, R), BF16), v((C, R), BF16), v((D, C, R), BF16),
        v((D, R, R), BF16), v((8, R, R), BF16), v((N, R), BF16), v((8, C, R), BF16), v((D, C, R), BF16),
        v((K, K), BF16), v((K, K), BF16), v((K, K), F32), v((D, C, K), BF16), v((D, C, K), BF16), v((C, K), BF16),
        v((8, C, K), BF16), v((C, K), BF16), v((D, C, K), BF16), v((D, C, K), BF16), v((2, K, K), F32),
        dma((9,)), dma((2,)), dma((2,)), *[dma((D,))] * 6, dma((D,)), dma((D,)), dma((8,)), dma((8,)),
        *[dma((D,))] * 4, dma((5,)),
    ]
    return pl.pallas_call(
        kernel,
        out_shape=(jax.ShapeDtypeStruct((N, K), BF16), jax.ShapeDtypeStruct((K, K), F32), jax.ShapeDtypeStruct((K, K), F32)),
        in_specs=[any_spec] * 9 + [pl.BlockSpec(memory_space=pltpu.SMEM)],
        out_specs=(any_spec, any_spec, any_spec),
        scratch_shapes=scratch,
        compiler_params=pltpu.CompilerParams(
            collective_id=0, has_side_effects=True, vmem_limit_bytes=60 * 1024 * 1024),
    )(*args)


def solution(mesh):
    in_specs = (
        P(GRP_LEAF, None), P(GRP_LEAF, None), P(GRP_LEAF, None), P(GRP_LEAF, None, None), P(GRP_LEAF, None, None),
        P(GRP_LEAF, None, None), P(None, GRP_LEAF, None, None), P(None, "grp", None, None), P(), P(),
    )
    return jax.shard_map(
        body, mesh=mesh, in_specs=in_specs, out_specs=(P(GRP_LEAF, None), P(), P()), check_vma=False)
```

```python
import jax
import jax.numpy as jnp
from jax import lax
from jax.experimental import pallas as pl
from jax.experimental.pallas import tpu as pltpu
from jax.sharding import PartitionSpec as P

F32 = jnp.float32
BF16 = jnp.bfloat16
GRP_LEAF = ("grp", "leaf")
N = 1536
R = 128
K = 256
D = 16
C = K // D


def mm(a, b):
    return lax.dot_general(a, b, (((1,), (0,)), ((), ())), preferred_element_type=F32)


def mmt(a, b):
    return lax.dot_general(a, b, (((1,), (1,)), ((), ())), preferred_element_type=F32)


def kernel(
    x_h, res_h, ord_h, diag_h, up_h, dn_h, lop_h, iop_h, top_h, ridge_s,
    img_v, out_v,
    x_v, res_v, ord_v, diag_v, up_v, dn_v, lop_v, iop_v, w_v, rp_v, bp_v,
    p_v, pt_v, og_v, xt_v, loc_v, im_v,
    s0_v, sib_v, l1_v, a_r, root_v, b_r, t_v, q_v, vr_v, xv_v, c_v, c_r,
    pre_v, gs_v, gs_r, h_v, h_r, z_v, z_r, f_v, f_r, o_r,
    load_sem, pair_s, pair_r, a_ss, a_rs, b_ss, b_rs, c_ss, c_rs,
    h_ss, h_rs, z_ss, z_rs, f_ss, f_rs, o_ss, o_rs,
):
    me = lax.axis_index("leaf")
    g = lax.axis_index("grp")
    core = lax.rem(me, 2)
    z = me // 2
    sibling = me + 1 - 2 * core

    leaf_peers = [lax.rem(me + r, D) for r in sorted(range(1, D), key=lambda r: -min(r, D - r))]
    z_peers = [lax.rem(me + 2 * r, D) for r in sorted(range(1, D // 2), key=lambda r: -min(r, D // 2 - r))]
    steps = sorted(((dy, dx) for dy in range(4) for dx in range(4) if dy or dx),
                   key=lambda s: -(min(s[0], 4 - s[0]) + min(s[1], 4 - s[1])))
    gy, gx = g // 4, lax.rem(g, 4)
    grp_peers = [lax.rem(gy + dy, 4) * 4 + lax.rem(gx + dx, 4) for dy, dx in steps]

    def sib_of(a):
        return a + 1 - 2 * lax.rem(a, 2)

    def remote(axis, src, dst, ss, rs, j):
        return pltpu.make_async_remote_copy(
            src_ref=src, dst_ref=dst, send_sem=ss, recv_sem=rs,
            device_id={axis: j}, device_id_type=pl.DeviceIdType.MESH)

    a4, a5, a6, a7 = g, g // 2, g // 4, g // 8
    pairs = [
        (ord_h, ord_v), (up_h.at[0], up_v), (lop_h.at[:, 0], lop_v), (x_h, x_v),
        (iop_h, iop_v), (top_h.at[0, 0:28], w_v),
        (top_h.at[1, a4], rp_v.at[0]), (top_h.at[1, 16 + a5], rp_v.at[1]), (top_h.at[1, 24 + a6], rp_v.at[2]),
        (top_h.at[2, a4], bp_v.at[0]), (top_h.at[2, 16 + a5], bp_v.at[1]), (top_h.at[2, 24 + a6], bp_v.at[2]),
        (top_h.at[2, 28 + a7], bp_v.at[3]),
        (dn_h.at[0], dn_v), (diag_h.at[0], diag_v), (res_h, res_v),
    ]
    loads = [pltpu.make_async_copy(src, dst, load_sem.at[i]) for i, (src, dst) in enumerate(pairs)]
    l_ord, l_up, l_lop, l_x, l_iop = loads[:5]
    l_top = loads[5:13]
    l_dn, l_diag, l_res = loads[13:]
    for copy in loads[:4]:
        copy.start()

    barrier = pltpu.get_barrier_semaphore()
    for j in leaf_peers:
        pl.semaphore_signal(barrier, inc=1, device_id={"leaf": j}, device_id_type=pl.DeviceIdType.MESH)
    for j in grp_peers:
        pl.semaphore_signal(barrier, inc=1, device_id={"grp": j}, device_id_type=pl.DeviceIdType.MESH)

    l_ord.wait()
    order = ord_v[...]
    column = jnp.broadcast_to(order.astype(F32), (R, N)).T.astype(jnp.int32)
    lane = lax.broadcasted_iota(jnp.int32, (N, R), 1)
    low = jnp.where((column & (R - 1)) == lane, 1.0, 0.0).astype(BF16)
    high = (column >> 7).astype(BF16)
    for j in range(N // R):
        p_v[:, j * R:(j + 1) * R] = jnp.where(high == jnp.asarray(j, BF16), low, jnp.zeros_like(low))

    l_up.wait()
    l_lop.wait()
    up_t = up_v[...].T
    lift_t = lax.dot_general(lop_v[0], up_t, (((0,), (0,)), ((), ())), preferred_element_type=F32).astype(BF16)
    both_t = jnp.concatenate([up_t, lift_t], axis=0)

    l_x.wait()
    for copy in loads[4:]:
        copy.start()
    for t in range(3):
        rows = pl.ds(t * 512, 512)
        og_v[rows, :] = mm(p_v[rows, :], x_v[...]).astype(BF16)
    both = mm(both_t, og_v[...]).T
    s0_v[...] = both[:, :R].astype(BF16)
    l1_v[...] = both[:, R:].astype(BF16).reshape(D, C, R)

    pl.semaphore_wait(barrier, 2 * (D - 1))

    sends = []

    def send(*args):
        copy = remote(*args)
        copy.start()
        sends.append(copy)
        return copy

    for i, j in enumerate(leaf_peers):
        send("leaf", l1_v.at[j], a_r.at[me], a_ss.at[i], a_rs.at[me], j)
    pair = send("leaf", s0_v, sib_v, pair_s.at[0], pair_r.at[0], sibling)
    a_r[me] = l1_v[me]

    l_iop.wait()
    up2 = [mm(iop_v[0, 8 + 2 * m:10 + 2 * m].reshape(2 * R, R), iop_v[0, 12 + m]).astype(BF16) for m in range(2)]
    up1 = [mm(iop_v[0, 2 * m:2 * m + 2].reshape(2 * R, R), up2[m // 2][(m % 2) * R:(m % 2 + 1) * R]).astype(BF16)
           for m in range(4)]
    q2 = [mm(iop_v[1, 8 + m], iop_v[1, 12 + m // 2]).astype(BF16) for m in range(4)]
    for m in range(8):
        q_v[m] = mm(iop_v[1, m], q2[m // 2]).astype(BF16)
    for copy in l_top:
        copy.wait()
    y5 = rp_v[0]
    y6 = mm(y5, rp_v[1]).astype(BF16)
    y7 = mm(y6, rp_v[2]).astype(BF16)
    x5 = mm(y5, bp_v[1]).astype(BF16)
    x6 = mm(y6, bp_v[2]).astype(BF16)
    x7 = mm(y7, bp_v[3]).astype(BF16)

    def lifts(base, node, count):
        return w_v[pl.ds(base + node, count)].reshape(count * R, R)

    t_v[g] = jnp.zeros((R, R), BF16)
    n4, n5, n6, n7 = sib_of(a4), sib_of(a5), sib_of(a6), sib_of(a7)
    t_v[n4] = bp_v[0].T
    t_v[pl.ds(2 * n5, 2)] = mmt(lifts(0, 2 * n5, 2), x5).astype(BF16).reshape(2, R, R)
    w = mmt(lifts(16, 2 * n6, 2), x6).astype(BF16)
    for b in range(2):
        t_v[pl.ds(4 * n6 + 2 * b, 2)] = mm(lifts(0, 4 * n6 + 2 * b, 2), w[b * R:(b + 1) * R]).astype(BF16).reshape(2, R, R)
    w = mmt(lifts(24, 2 * n7, 2), x7).astype(BF16)
    for b in range(2):
        u = mm(lifts(16, 4 * n7 + 2 * b, 2), w[b * R:(b + 1) * R]).astype(BF16)
        for d in range(2):
            first = 8 * n7 + 4 * b + 2 * d
            t_v[pl.ds(first, 2)] = mm(lifts(0, first, 2), u[d * R:(d + 1) * R]).astype(BF16).reshape(2, R, R)

    row_low = jnp.broadcast_to(order & (R - 1), (R, N))
    row_high = jnp.broadcast_to(order >> 7, (R, N)).astype(F32).astype(BF16)
    row_one = jnp.where(row_low == lax.broadcasted_iota(jnp.int32, (R, N), 0), 1.0, 0.0).astype(BF16)
    for j in range(N // R):
        pt_v[j * R:(j + 1) * R, :] = jnp.where(row_high == jnp.asarray(j, BF16), row_one, jnp.zeros_like(row_one))
    l_dn.wait()
    vr_v[...] = mm(dn_v[...], lop_v[1]).astype(BF16)
    xt_v[:K, :] = og_v[...].T
    l_diag.wait()
    ridge = ridge_s[0]
    for t in range(3):
        rows = pl.ds(t * 512, 512)
        loc_v[rows, :] = mm(diag_v[rows, :], og_v[...]) + ridge * og_v[rows, :].astype(F32)

    for i, j in enumerate(leaf_peers):
        remote("leaf", l1_v.at[j], a_r.at[j], a_ss.at[i], a_rs.at[j], j).wait_recv()
    s1 = [(a_r[2 * m].astype(F32) + a_r[2 * m + 1].astype(F32)).astype(BF16) for m in range(8)]
    s1p = [jnp.concatenate(s1[2 * m:2 * m + 2], axis=1) for m in range(4)]
    root = mm(s1p[0], up1[0])
    for m in range(1, 4):
        root = root + mm(s1p[m], up1[m])
    root_v[...] = root.astype(BF16)

    for i, j in enumerate(grp_peers):
        send("grp", root_v, b_r.at[g], b_ss.at[i], b_rs.at[g], j)
    b_r[g] = root_v[...]

    s2 = [mm(s1p[m], iop_v[0, 2 * m:2 * m + 2].reshape(2 * R, R)).astype(BF16) for m in range(4)]
    s2p = [jnp.concatenate(s2[2 * m:2 * m + 2], axis=1) for m in range(2)]
    s3 = [mm(s2p[m], iop_v[0, 8 + 2 * m:10 + 2 * m].reshape(2 * R, R)).astype(BF16) for m in range(2)]
    c3 = [mmt(s3[1 - m], iop_v[2, 12 + m]).astype(BF16) for m in range(2)]
    c2 = [(mmt(s2[m ^ 1], iop_v[2, 8 + m]) + mmt(c3[m // 2], iop_v[1, 8 + m])).astype(BF16) for m in range(4)]
    c1 = [mmt(s1[m ^ 1], iop_v[2, m]) + mmt(c2[m // 2], iop_v[1, m]) for m in range(8)]
    pair.wait_recv()
    near = mmt(sib_v[...], lop_v[2]).astype(BF16)
    loc_v[...] = loc_v[...] + mmt(dn_v[...], near)
    l_res.wait()
    for t in range(3):
        rows = pl.ds(t * 512, 512)
        xt_v[K:, rows] = mm(p_v[rows, :], res_v[...]).astype(BF16).T

    for i, j in enumerate(grp_peers):
        remote("grp", root_v, b_r.at[j], b_ss.at[i], b_rs.at[j], j).wait_recv()
    c4 = jnp.zeros((C, R), F32)
    for m in range(D // 2):
        c4 = c4 + mm(jnp.concatenate([b_r[2 * m], b_r[2 * m + 1]], axis=1), t_v[2 * m:2 * m + 2].reshape(2 * R, R))
    c4 = c4.astype(BF16)
    for m in range(8):
        c_v[m] = (c1[m] + mmt(c4, q_v[m])).astype(BF16)

    for i, j in enumerate(leaf_peers):
        send("leaf", c_v.at[j // 2], c_r.at[me], c_ss.at[i], c_rs.at[me], j)
    c_r[me] = c_v[z]

    im_v[...] = loc_v[...].astype(BF16)
    for t in range(2):
        pre_v[t] = mm(xt_v[t * K:(t + 1) * K, :], im_v[...])
    xv_v[...] = mm(xt_v[...], vr_v[...]).astype(BF16).reshape(2, K, R)

    for i, j in enumerate(leaf_peers):
        remote("leaf", c_v.at[j // 2], c_r.at[j], c_ss.at[i], c_rs.at[j], j).wait_recv()

    coarse = c_r[...].reshape(K, R)
    gs_v[...] = (pre_v[1 - core] + mmt(xv_v[1 - core], coarse)).astype(BF16)
    swap = send("leaf", gs_v, gs_r, pair_s.at[1], pair_r.at[1], sibling)
    own = pre_v[core] + mmt(xv_v[core], coarse)
    im_v[...] = (loc_v[...] + mmt(vr_v[...], coarse)).astype(BF16)
    swap.wait_recv()
    h_v[...] = (own + gs_r[...].astype(F32)).astype(BF16).reshape(D, C, K)
    for i, j in enumerate(grp_peers):
        send("grp", h_v.at[j], h_r.at[g], h_ss.at[i], h_rs.at[g], j)
    h_r[g] = h_v[g]

    for t in range(3):
        rows = pl.ds(t * 512, 512)
        img_v[rows, :] = mm(pt_v[rows, :], im_v[...]).astype(BF16)

    for i, j in enumerate(grp_peers):
        remote("grp", h_v.at[j], h_r.at[j], h_ss.at[i], h_rs.at[j], j).wait_recv()
    total = h_r[0].astype(F32)
    for j in range(1, D):
        total = total + h_r[j].astype(F32)
    z_v[...] = total.astype(BF16)
    for i, j in enumerate(z_peers):
        send("leaf", z_v, z_r.at[z], z_ss.at[i], z_rs.at[z], j)
    z_r[z] = z_v[...]
    for i, j in enumerate(z_peers):
        remote("leaf", z_v, z_r.at[j // 2], z_ss.at[i], z_rs.at[j // 2], j).wait_recv()
    total = z_r[0].astype(F32)
    for j in range(1, D // 2):
        total = total + z_r[j].astype(F32)
    f_v[...] = total.astype(BF16)
    for i, j in enumerate(grp_peers):
        send("grp", f_v, f_r.at[g], f_ss.at[i], f_rs.at[g], j)
    f_r[g] = f_v[...]
    send("leaf", f_v, o_r.at[g], o_ss.at[g], o_rs.at[g], sibling)
    for i, j in reversed(list(enumerate(grp_peers))):
        remote("grp", f_v, f_r.at[j], f_ss.at[i], f_rs.at[j], j).wait_recv()
        send("leaf", f_r.at[j], o_r.at[j], o_ss.at[j], o_rs.at[j], sibling)
    scale = 1.0 / (N * D * D)
    out_v[core] = f_r[...].reshape(K, K).astype(F32) * scale
    for j in range(D):
        remote("leaf", f_r.at[j], o_r.at[j], o_ss.at[j], o_rs.at[j], sibling).wait_recv()
    out_v[1 - core] = o_r[...].reshape(K, K).astype(F32) * scale
    for copy in sends:
        copy.wait_send()


def finish(image, grams, img_h, cur_h, cor_h, sem):
    copies = [
        pltpu.make_async_copy(src, dst, sem.at[i])
        for i, (src, dst) in enumerate(((image, img_h), (grams.at[0], cur_h), (grams.at[1], cor_h)))
    ]
    for copy in copies:
        copy.start()
    for copy in copies:
        copy.wait()


def body(*args):
    any_spec = pl.BlockSpec(memory_space=pl.ANY)
    vmem_spec = pl.BlockSpec(memory_space=pltpu.VMEM)
    dma = pltpu.SemaphoreType.DMA
    v = pltpu.VMEM
    scratch = [
        v((N, K), BF16), v((N, K), BF16), v((1, N), jnp.int32), v((N, N), BF16), v((N, R), BF16), v((N, R), BF16),
        v((3, R, R), BF16), v((3, 14, R, R), BF16), v((28, R, R), BF16), v((3, R, R), BF16), v((4, R, R), BF16),
        v((N, N), BF16), v((N, N), BF16), v((N, K), BF16), v((2 * K, N), BF16), v((N, K), F32), v((N, K), BF16),
        v((K, R), BF16), v((K, R), BF16), v((D, C, R), BF16), v((D, C, R), BF16), v((C, R), BF16), v((D, C, R), BF16),
        v((D, R, R), BF16), v((8, R, R), BF16), v((N, R), BF16), v((2, K, R), BF16), v((8, C, R), BF16), v((D, C, R), BF16),
        v((2, K, K), F32), v((K, K), BF16), v((K, K), BF16), v((D, C, K), BF16), v((D, C, K), BF16), v((C, K), BF16),
        v((8, C, K), BF16), v((C, K), BF16), v((D, C, K), BF16), v((D, C, K), BF16),
        dma((16,)), dma((2,)), dma((2,)), *[dma((D,))] * 6, dma((D,)), dma((D,)), dma((8,)), dma((8,)), *[dma((D,))] * 4,
    ]
    args = [pltpu.with_memory_space_constraint(a, pltpu.HBM) for a in args[:-1]] + [args[-1]]
    image, grams = pl.pallas_call(
        kernel,
        out_shape=(jax.ShapeDtypeStruct((N, K), BF16), jax.ShapeDtypeStruct((2, K, K), F32)),
        in_specs=[any_spec] * 9 + [pl.BlockSpec(memory_space=pltpu.SMEM)],
        out_specs=(vmem_spec, vmem_spec),
        scratch_shapes=scratch,
        compiler_params=pltpu.CompilerParams(
            collective_id=0, has_side_effects=True, vmem_limit_bytes=48 * 1024 * 1024),
    )(*args)
    return pl.pallas_call(
        finish,
        out_shape=(jax.ShapeDtypeStruct((N, K), BF16), jax.ShapeDtypeStruct((K, K), F32), jax.ShapeDtypeStruct((K, K), F32)),
        in_specs=[any_spec, any_spec],
        out_specs=(any_spec, any_spec, any_spec),
        scratch_shapes=[dma((3,))],
        compiler_params=pltpu.CompilerParams(vmem_limit_bytes=1024 * 1024),
    )(image, grams)


def solution(mesh):
    in_specs = (
        P(GRP_LEAF, None), P(GRP_LEAF, None), P(GRP_LEAF, None), P(GRP_LEAF, None, None), P(GRP_LEAF, None, None),
        P(GRP_LEAF, None, None), P(None, GRP_LEAF, None, None), P(None, "grp", None, None), P(), P(),
    )
    return jax.shard_map(
        body, mesh=mesh, in_specs=in_specs, out_specs=(P(GRP_LEAF, None), P(), P()), check_vma=False)
```

```python
import jax
import jax.numpy as jnp
from jax import lax
from jax.experimental import pallas as pl
from jax.experimental.pallas import tpu as pltpu
from jax.sharding import PartitionSpec as P

F32 = jnp.float32
BF16 = jnp.bfloat16
GRP_LEAF = ("grp", "leaf")
N = 1536
R = 128
K = 256
D = 16
C = K // D


def mm(a, b):
    return lax.dot_general(a, b, (((1,), (0,)), ((), ())), preferred_element_type=F32)


def mmt(a, b):
    return lax.dot_general(a, b, (((1,), (1,)), ((), ())), preferred_element_type=F32)


def kernel(
    x_h, res_h, ord_h, diag_h, up_h, dn_h, lop_h, iop_h, top_h, ridge_s,
    img_v, out_v,
    x_v, res_v, ord_v, diag_v, up_v, dn_v, lop_v, iop_v, w_v, path_v,
    p_v, pt_v, og_v, xt_v, loc_v, im_v,
    s0_v, sib_v, l1_v, a_r, root_v, b_r, t_v, u_v, q_v, vr_v, xv_v, c_v, c_r,
    pre_v, gs_v, gs_r, h_v, h_r, z_v, z_r, f_v, f_r, o_r,
    load_sem, send_sem, recv_sem,
):
    me = lax.axis_index("leaf")
    g = lax.axis_index("grp")
    core = lax.rem(me, 2)
    z = me // 2
    sibling = me + 1 - 2 * core

    leaf_peers = [lax.rem(me + r, D) for r in sorted(range(1, D), key=lambda r: -min(r, D - r))]
    z_peers = [lax.rem(me + 2 * r, D) for r in sorted(range(1, D // 2), key=lambda r: -min(r, D // 2 - r))]
    steps = sorted(((dy, dx) for dy in range(4) for dx in range(4) if dy or dx),
                   key=lambda s: -(min(s[0], 4 - s[0]) + min(s[1], 4 - s[1])))
    gy, gx = g // 4, lax.rem(g, 4)
    grp_peers = [lax.rem(gy + dy, 4) * 4 + lax.rem(gx + dx, 4) for dy, dx in steps]

    def sib_of(a):
        return a + 1 - 2 * lax.rem(a, 2)

    def remote(phase, axis, src, dst, j):
        return pltpu.make_async_remote_copy(
            src_ref=src, dst_ref=dst, send_sem=send_sem.at[phase], recv_sem=recv_sem.at[phase],
            device_id={axis: j}, device_id_type=pl.DeviceIdType.MESH)

    def arrived(phase, ref):
        remote(phase, "leaf", ref, ref, sibling).wait_recv()

    def left(phase, ref):
        remote(phase, "leaf", ref, ref, sibling).wait_send()

    a4, a5, a6, a7 = g, g // 2, g // 4, g // 8
    def start_all(copies):
        for copy in copies:
            copy.start()

    def load(slot, src, dst):
        return pltpu.make_async_copy(src, dst, load_sem.at[slot])

    l_ord = load(0, ord_h, ord_v)
    l_up = load(1, up_h.at[0], up_v)
    l_lop = load(2, lop_h.at[:, 0], lop_v)
    l_x = load(3, x_h, x_v)
    start_all([l_ord, l_up, l_lop, l_x])
    l_iop = load(4, iop_h, iop_v)
    l_lift = load(5, top_h.at[0, 0:28], w_v)
    path = [(1, a4), (1, 16 + a5), (1, 24 + a6), (2, a4), (2, 16 + a5), (2, 24 + a6), (2, 28 + a7)]
    l_path = [load(6, top_h.at[kind, node], path_v.at[i]) for i, (kind, node) in enumerate(path)]
    l_dn = load(7, dn_h.at[0], dn_v)
    l_diag = load(8, diag_h.at[0], diag_v)
    l_res = load(9, res_h, res_v)

    barrier = pltpu.get_barrier_semaphore()
    for j in leaf_peers:
        pl.semaphore_signal(barrier, inc=1, device_id={"leaf": j}, device_id_type=pl.DeviceIdType.MESH)
    for j in grp_peers:
        pl.semaphore_signal(barrier, inc=1, device_id={"grp": j}, device_id_type=pl.DeviceIdType.MESH)

    l_ord.wait()
    order = ord_v[...]
    column = jnp.broadcast_to(order.astype(F32), (R, N)).T.astype(jnp.int32)
    lane = lax.broadcasted_iota(jnp.int32, (N, R), 1)
    low = jnp.where((column & (R - 1)) == lane, 1.0, 0.0).astype(BF16)
    high = (column >> 7).astype(BF16)
    for j in range(N // R):
        p_v[:, j * R:(j + 1) * R] = jnp.where(high == jnp.asarray(j, BF16), low, jnp.zeros_like(low))

    l_up.wait()
    l_lop.wait()
    up_t = up_v[...].T
    lift_t = lax.dot_general(lop_v[0], up_t, (((0,), (0,)), ((), ())), preferred_element_type=F32).astype(BF16)
    both_t = jnp.concatenate([up_t, lift_t], axis=0)

    both_t = mm(both_t, p_v[...]).astype(BF16)
    l_x.wait()
    start_all([l_iop, l_lift, *l_path, l_dn, l_diag, l_res])
    both = mm(both_t, x_v[...]).T
    s0_v[...] = both[:, :R].astype(BF16)
    l1_v[...] = both[:, R:].astype(BF16).reshape(D, C, R)

    pl.semaphore_wait(barrier, 2 * (D - 1))

    for j in leaf_peers:
        remote(0, "leaf", l1_v.at[j], a_r.at[me], j).start()
    remote(1, "leaf", s0_v, sib_v, sibling).start()
    a_r[me] = l1_v[me]

    for t in range(3):
        rows = pl.ds(t * 512, 512)
        og_v[rows, :] = mm(p_v[rows, :], x_v[...]).astype(BF16)
    l_iop.wait()
    up2 = [mm(iop_v[0, 8 + 2 * m:10 + 2 * m].reshape(2 * R, R), iop_v[0, 12 + m]).astype(BF16) for m in range(2)]
    for m in range(4):
        u_v[2 * R * m:2 * R * (m + 1), :] = mm(
            iop_v[0, 2 * m:2 * m + 2].reshape(2 * R, R), up2[m // 2][(m % 2) * R:(m % 2 + 1) * R]).astype(BF16)
    q2 = [mm(iop_v[1, 8 + m], iop_v[1, 12 + m // 2]).astype(BF16) for m in range(4)]
    for m in range(8):
        q_v[m * R:(m + 1) * R, :] = mm(iop_v[1, m], q2[m // 2]).astype(BF16)
    l_lift.wait()
    load(6, top_h.at[1, 0:7], path_v).wait()
    y5 = path_v[0]
    y6 = mm(y5, path_v[1]).astype(BF16)
    y7 = mm(y6, path_v[2]).astype(BF16)
    x5 = mm(y5, path_v[4]).astype(BF16)
    x6 = mm(y6, path_v[5]).astype(BF16)
    x7 = mm(y7, path_v[6]).astype(BF16)

    def lifts(base, node, count):
        return w_v[pl.ds(base + node, count)].reshape(count * R, R)

    t_v[g] = jnp.zeros((R, R), BF16)
    n4, n5, n6, n7 = sib_of(a4), sib_of(a5), sib_of(a6), sib_of(a7)
    t_v[n4] = path_v[3].T
    t_v[pl.ds(2 * n5, 2)] = mmt(lifts(0, 2 * n5, 2), x5).astype(BF16).reshape(2, R, R)
    w = mmt(lifts(16, 2 * n6, 2), x6).astype(BF16)
    for b in range(2):
        t_v[pl.ds(4 * n6 + 2 * b, 2)] = mm(lifts(0, 4 * n6 + 2 * b, 2), w[b * R:(b + 1) * R]).astype(BF16).reshape(2, R, R)
    w = mmt(lifts(24, 2 * n7, 2), x7).astype(BF16)
    for b in range(2):
        u = mm(lifts(16, 4 * n7 + 2 * b, 2), w[b * R:(b + 1) * R]).astype(BF16)
        for d in range(2):
            first = 8 * n7 + 4 * b + 2 * d
            t_v[pl.ds(first, 2)] = mm(lifts(0, first, 2), u[d * R:(d + 1) * R]).astype(BF16).reshape(2, R, R)

    row_low = jnp.broadcast_to(order & (R - 1), (R, N))
    row_high = jnp.broadcast_to(order >> 7, (R, N)).astype(F32).astype(BF16)
    row_one = jnp.where(row_low == lax.broadcasted_iota(jnp.int32, (R, N), 0), 1.0, 0.0).astype(BF16)
    for j in range(N // R):
        pt_v[j * R:(j + 1) * R, :] = jnp.where(row_high == jnp.asarray(j, BF16), row_one, jnp.zeros_like(row_one))
    l_dn.wait()
    vr_v[...] = mm(dn_v[...], lop_v[1]).astype(BF16)
    xt_v[:K, :] = og_v[...].T
    l_diag.wait()
    ridge = ridge_s[0]
    for t in range(3):
        rows = pl.ds(t * 512, 512)
        loc_v[rows, :] = mm(diag_v[rows, :], og_v[...]) + ridge * og_v[rows, :].astype(F32)

    arrived(0, a_r.at[0:15])
    s1 = [(a_r[2 * m].astype(F32) + a_r[2 * m + 1].astype(F32)).astype(BF16) for m in range(8)]
    s1p = [jnp.concatenate(s1[2 * m:2 * m + 2], axis=1) for m in range(4)]
    root_v[...] = mm(jnp.concatenate(s1, axis=1), u_v[...]).astype(BF16)

    for j in grp_peers:
        remote(2, "grp", root_v, b_r.at[g], j).start()
    b_r[g] = root_v[...]

    s2 = [mm(s1p[m], iop_v[0, 2 * m:2 * m + 2].reshape(2 * R, R)).astype(BF16) for m in range(4)]
    s2p = [jnp.concatenate(s2[2 * m:2 * m + 2], axis=1) for m in range(2)]
    s3 = [mm(s2p[m], iop_v[0, 8 + 2 * m:10 + 2 * m].reshape(2 * R, R)).astype(BF16) for m in range(2)]
    c3 = [mmt(s3[1 - m], iop_v[2, 12 + m]).astype(BF16) for m in range(2)]
    c2 = [(mmt(s2[m ^ 1], iop_v[2, 8 + m]) + mmt(c3[m // 2], iop_v[1, 8 + m])).astype(BF16) for m in range(4)]
    c1 = [mmt(s1[m ^ 1], iop_v[2, m]) + mmt(c2[m // 2], iop_v[1, m]) for m in range(8)]
    arrived(1, sib_v)
    near = mmt(sib_v[...], lop_v[2]).astype(BF16)
    loc_v[...] = loc_v[...] + mmt(dn_v[...], near)
    l_res.wait()
    for t in range(3):
        rows = pl.ds(t * 512, 512)
        xt_v[K:, rows] = mm(p_v[rows, :], res_v[...]).astype(BF16).T

    arrived(2, b_r.at[0:15])
    c4 = mm(jnp.concatenate([b_r[j] for j in range(D)], axis=1), t_v[...].reshape(D * R, R)).astype(BF16)
    down = mmt(c4, q_v[...])
    for m in range(8):
        c_v[m] = (c1[m] + down[:, m * R:(m + 1) * R]).astype(BF16)

    for j in z_peers:
        remote(3, "leaf", c_v.at[j // 2], c_r.at[z, core], j).start()
    c_r[z, core] = c_v[z]

    im_v[...] = loc_v[...].astype(BF16)
    for t in range(2):
        pre_v[t] = mm(xt_v[t * K:(t + 1) * K, :], im_v[...])
    xv_v[...] = mm(xt_v[...], vr_v[...]).astype(BF16).reshape(2, K, R)

    arrived(3, c_v.at[0:7])
    remote(4, "leaf", c_r.at[:, core], c_r.at[:, core], sibling).start()
    arrived(4, c_v)

    coarse = c_r[...].reshape(K, R)
    gs_v[...] = (pre_v[1 - core] + mmt(xv_v[1 - core], coarse)).astype(BF16)
    remote(5, "leaf", gs_v, gs_r, sibling).start()
    own = pre_v[core] + mmt(xv_v[core], coarse)
    im_v[...] = (loc_v[...] + mmt(vr_v[...], coarse)).astype(BF16)
    arrived(5, gs_r)
    h_v[...] = (own + gs_r[...].astype(F32)).astype(BF16).reshape(D, C, K)
    for j in grp_peers:
        remote(6, "grp", h_v.at[j], h_r.at[g], j).start()
    h_r[g] = h_v[g]

    for t in range(3):
        rows = pl.ds(t * 512, 512)
        img_v[rows, :] = mm(pt_v[rows, :], im_v[...]).astype(BF16)

    arrived(6, h_r.at[0:15])
    total = h_r[0].astype(F32)
    for j in range(1, D):
        total = total + h_r[j].astype(F32)
    z_v[...] = total.astype(BF16)
    for j in z_peers:
        remote(7, "leaf", z_v, z_r.at[z], j).start()
    z_r[z] = z_v[...]
    arrived(7, z_r.at[0:7])
    total = z_r[0].astype(F32)
    for j in range(1, D // 2):
        total = total + z_r[j].astype(F32)
    f_v[...] = total.astype(BF16)
    for j in grp_peers:
        remote(8, "grp", f_v, f_r.at[g], j).start()
    f_r[g] = f_v[...]
    arrived(8, f_r.at[0:15])
    remote(9, "leaf", f_r, o_r, sibling).start()
    scale = 1.0 / (N * D * D)
    out_v[core] = f_r[...].reshape(K, K).astype(F32) * scale
    arrived(9, o_r)
    out_v[1 - core] = o_r[...].reshape(K, K).astype(F32) * scale
    for phase, ref in enumerate((
        l1_v.at[0:15], s0_v, b_r.at[0:15], c_v.at[0:7], c_v, gs_v, h_v.at[0:15], z_r.at[0:7], f_r.at[0:15], f_r,
    )):
        left(phase, ref)


def finish(image, grams, img_h, cur_h, cor_h, sem):
    rows = [pl.ds(t * 256, 256) for t in range(N // 256)]
    pairs = [(image.at[r], img_h.at[r]) for r in rows]
    pairs += [(grams.at[i, pl.ds(t * 128, 128)], dst.at[pl.ds(t * 128, 128)]) for i, dst in enumerate((cur_h, cor_h)) for t in range(2)]
    copies = [pltpu.make_async_copy(src, dst, sem.at[i]) for i, (src, dst) in enumerate(pairs)]
    for copy in copies:
        copy.start()
    for copy in copies:
        copy.wait()


def body(*args):
    any_spec = pl.BlockSpec(memory_space=pl.ANY)
    vmem_spec = pl.BlockSpec(memory_space=pltpu.VMEM)
    dma = pltpu.SemaphoreType.DMA
    v = pltpu.VMEM
    scratch = [
        v((N, K), BF16), v((N, K), BF16), v((1, N), jnp.int32), v((N, N), BF16), v((N, R), BF16), v((N, R), BF16),
        v((3, R, R), BF16), v((3, 14, R, R), BF16), v((28, R, R), BF16), v((7, R, R), BF16),
        v((N, N), BF16), v((N, N), BF16), v((N, K), BF16), v((2 * K, N), BF16), v((N, K), F32), v((N, K), BF16),
        v((K, R), BF16), v((K, R), BF16), v((D, C, R), BF16), v((D, C, R), BF16), v((C, R), BF16), v((D, C, R), BF16),
        v((D, R, R), BF16), v((8 * R, R), BF16), v((8 * R, R), BF16), v((N, R), BF16), v((2, K, R), BF16), v((8, C, R), BF16), v((8, 2, C, R), BF16),
        v((2, K, K), F32), v((K, K), BF16), v((K, K), BF16), v((D, C, K), BF16), v((D, C, K), BF16), v((C, K), BF16),
        v((8, C, K), BF16), v((C, K), BF16), v((D, C, K), BF16), v((D, C, K), BF16),
        dma((10,)), dma((10,)), dma((10,)),
    ]
    args = [pltpu.with_memory_space_constraint(a, pltpu.HBM) for a in args[:-1]] + [args[-1]]
    image, grams = pl.pallas_call(
        kernel,
        out_shape=(jax.ShapeDtypeStruct((N, K), BF16), jax.ShapeDtypeStruct((2, K, K), F32)),
        in_specs=[any_spec] * 9 + [pl.BlockSpec(memory_space=pltpu.SMEM)],
        out_specs=(vmem_spec, vmem_spec),
        scratch_shapes=scratch,
        compiler_params=pltpu.CompilerParams(
            collective_id=0, has_side_effects=True, vmem_limit_bytes=48 * 1024 * 1024),
    )(*args)
    return pl.pallas_call(
        finish,
        out_shape=(jax.ShapeDtypeStruct((N, K), BF16), jax.ShapeDtypeStruct((K, K), F32), jax.ShapeDtypeStruct((K, K), F32)),
        in_specs=[any_spec, any_spec],
        out_specs=(any_spec, any_spec, any_spec),
        scratch_shapes=[dma((10,))],
        compiler_params=pltpu.CompilerParams(vmem_limit_bytes=1024 * 1024),
    )(image, grams)


def solution(mesh):
    in_specs = (
        P(GRP_LEAF, None), P(GRP_LEAF, None), P(GRP_LEAF, None), P(GRP_LEAF, None, None), P(GRP_LEAF, None, None),
        P(GRP_LEAF, None, None), P(None, GRP_LEAF, None, None), P(None, "grp", None, None), P(), P(),
    )
    return jax.shard_map(
        body, mesh=mesh, in_specs=in_specs, out_specs=(P(GRP_LEAF, None), P(), P()), check_vma=False)
```

```python
import jax
import jax.numpy as jnp
from jax import lax
from jax.experimental import pallas as pl
from jax.experimental.pallas import tpu as pltpu
from jax.sharding import PartitionSpec as P

F32 = jnp.float32
BF16 = jnp.bfloat16
GRP_LEAF = ("grp", "leaf")
N = 1536
R = 128
K = 256
D = 16
C = K // D


def mm(a, b):
    return lax.dot_general(a, b, (((1,), (0,)), ((), ())), preferred_element_type=F32)


def mmt(a, b):
    return lax.dot_general(a, b, (((1,), (1,)), ((), ())), preferred_element_type=F32)


def kernel(
    x_h, res_h, ord_h, diag_h, up_h, dn_h, lop_h, iop_h, top_h, ridge_s,
    img_v, out_v,
    x_v, res_v, ord_v, diag_v, up_v, dn_v, lop_v, iop_v, w_v, path_v,
    p_v, pt_v, og_v, xt_v, loc_v, im_v,
    s0_v, sib_v, l1_v, a_r, root_v, b_r, t_v, u_v, q_v, vr_v, xv_v, c_v, c_r,
    pre_v, gs_v, gs_r, h_v, h_r, z_v, z_r, f_v, f_r, o_r,
    load_sem, send_sem, recv_sem,
):
    me = lax.axis_index("leaf")
    g = lax.axis_index("grp")
    core = lax.rem(me, 2)
    z = me // 2
    sibling = me + 1 - 2 * core

    leaf_peers = [lax.rem(me + r, D) for r in sorted(range(1, D), key=lambda r: -min(r, D - r))]
    z_peers = [lax.rem(me + 2 * r, D) for r in sorted(range(1, D // 2), key=lambda r: -min(r, D // 2 - r))]
    steps = sorted(((dy, dx) for dy in range(4) for dx in range(4) if dy or dx),
                   key=lambda s: -(min(s[0], 4 - s[0]) + min(s[1], 4 - s[1])))
    gy, gx = g // 4, lax.rem(g, 4)
    grp_peers = [lax.rem(gy + dy, 4) * 4 + lax.rem(gx + dx, 4) for dy, dx in steps]

    def sib_of(a):
        return a + 1 - 2 * lax.rem(a, 2)

    def remote(phase, axis, src, dst, j):
        return pltpu.make_async_remote_copy(
            src_ref=src, dst_ref=dst, send_sem=send_sem.at[phase], recv_sem=recv_sem.at[phase],
            device_id={axis: j}, device_id_type=pl.DeviceIdType.MESH)

    def arrived(phase, ref):
        remote(phase, "leaf", ref, ref, sibling).wait_recv()

    def left(phase, ref):
        remote(phase, "leaf", ref, ref, sibling).wait_send()

    a4, a5, a6, a7 = g, g // 2, g // 4, g // 8
    def start_all(copies):
        for copy in copies:
            copy.start()

    def load(slot, src, dst):
        return pltpu.make_async_copy(src, dst, load_sem.at[slot])

    l_ord = load(0, ord_h, ord_v)
    l_up = load(1, up_h.at[0], up_v)
    l_lop = load(2, lop_h.at[:, 0], lop_v)
    l_x = load(3, x_h, x_v)
    start_all([l_ord, l_up, l_lop, l_x])
    l_iop = load(4, iop_h, iop_v)
    l_lift = load(5, top_h.at[0, 0:28], w_v)
    path = [(1, a4), (1, 16 + a5), (1, 24 + a6), (2, a4), (2, 16 + a5), (2, 24 + a6), (2, 28 + a7)]
    l_path = [load(6, top_h.at[kind, node], path_v.at[i]) for i, (kind, node) in enumerate(path)]
    l_dn = load(7, dn_h.at[0], dn_v)
    l_diag = load(8, diag_h.at[0], diag_v)
    l_res = load(9, res_h, res_v)

    barrier = pltpu.get_barrier_semaphore()
    for j in leaf_peers:
        pl.semaphore_signal(barrier, inc=1, device_id={"leaf": j}, device_id_type=pl.DeviceIdType.MESH)
    for j in grp_peers:
        pl.semaphore_signal(barrier, inc=1, device_id={"grp": j}, device_id_type=pl.DeviceIdType.MESH)

    l_ord.wait()
    order = ord_v[...]
    column = jnp.broadcast_to(order.astype(F32), (R, N)).T.astype(jnp.int32)
    lane = lax.broadcasted_iota(jnp.int32, (N, R), 1)
    low = jnp.where((column & (R - 1)) == lane, 1.0, 0.0).astype(BF16)
    high = (column >> 7).astype(BF16)
    for j in range(N // R):
        p_v[:, j * R:(j + 1) * R] = jnp.where(high == jnp.asarray(j, BF16), low, jnp.zeros_like(low))

    l_up.wait()
    l_lop.wait()
    up_t = up_v[...].T
    lift_t = lax.dot_general(lop_v[0], up_t, (((0,), (0,)), ((), ())), preferred_element_type=F32).astype(BF16)
    both_t = jnp.concatenate([up_t, lift_t], axis=0)

    both_t = mm(both_t, p_v[...]).astype(BF16)
    l_x.wait()
    start_all([l_iop, l_lift, *l_path, l_dn, l_diag, l_res])
    both = mm(both_t, x_v[...]).T
    s0_v[...] = both[:, :R].astype(BF16)
    l1_v[...] = both[:, R:].astype(BF16).reshape(D, C, R)

    pl.semaphore_wait(barrier, 2 * (D - 1))

    for j in leaf_peers:
        remote(0, "leaf", l1_v.at[j], a_r.at[me], j).start()
    remote(1, "leaf", s0_v, sib_v, sibling).start()
    a_r[me] = l1_v[me]

    for t in range(3):
        rows = pl.ds(t * 512, 512)
        og_v[rows, :] = mm(p_v[rows, :], x_v[...]).astype(BF16)
    l_iop.wait()
    up2 = [mm(iop_v[0, 8 + 2 * m:10 + 2 * m].reshape(2 * R, R), iop_v[0, 12 + m]).astype(BF16) for m in range(2)]
    for m in range(4):
        u_v[2 * R * m:2 * R * (m + 1), :] = mm(
            iop_v[0, 2 * m:2 * m + 2].reshape(2 * R, R), up2[m // 2][(m % 2) * R:(m % 2 + 1) * R]).astype(BF16)
    q2 = [mm(iop_v[1, 8 + m], iop_v[1, 12 + m // 2]).astype(BF16) for m in range(4)]
    for m in range(8):
        q_v[m * R:(m + 1) * R, :] = mm(iop_v[1, m], q2[m // 2]).astype(BF16)
    l_lift.wait()
    load(6, top_h.at[1, 0:7], path_v).wait()
    y5 = path_v[0]
    y6 = mm(y5, path_v[1]).astype(BF16)
    y7 = mm(y6, path_v[2]).astype(BF16)
    x5 = mm(y5, path_v[4]).astype(BF16)
    x6 = mm(y6, path_v[5]).astype(BF16)
    x7 = mm(y7, path_v[6]).astype(BF16)

    def lifts(base, node, count):
        return w_v[pl.ds(base + node, count)].reshape(count * R, R)

    t_v[g] = jnp.zeros((R, R), BF16)
    n4, n5, n6, n7 = sib_of(a4), sib_of(a5), sib_of(a6), sib_of(a7)
    t_v[n4] = path_v[3].T
    t_v[pl.ds(2 * n5, 2)] = mmt(lifts(0, 2 * n5, 2), x5).astype(BF16).reshape(2, R, R)
    w = mmt(lifts(16, 2 * n6, 2), x6).astype(BF16)
    for b in range(2):
        t_v[pl.ds(4 * n6 + 2 * b, 2)] = mm(lifts(0, 4 * n6 + 2 * b, 2), w[b * R:(b + 1) * R]).astype(BF16).reshape(2, R, R)
    w = mmt(lifts(24, 2 * n7, 2), x7).astype(BF16)
    for b in range(2):
        u = mm(lifts(16, 4 * n7 + 2 * b, 2), w[b * R:(b + 1) * R]).astype(BF16)
        for d in range(2):
            first = 8 * n7 + 4 * b + 2 * d
            t_v[pl.ds(first, 2)] = mm(lifts(0, first, 2), u[d * R:(d + 1) * R]).astype(BF16).reshape(2, R, R)

    row_low = jnp.broadcast_to(order & (R - 1), (R, N))
    row_high = jnp.broadcast_to(order >> 7, (R, N)).astype(F32).astype(BF16)
    row_one = jnp.where(row_low == lax.broadcasted_iota(jnp.int32, (R, N), 0), 1.0, 0.0).astype(BF16)
    for j in range(N // R):
        pt_v[j * R:(j + 1) * R, :] = jnp.where(row_high == jnp.asarray(j, BF16), row_one, jnp.zeros_like(row_one))
    l_dn.wait()
    vr_v[...] = mm(dn_v[...], lop_v[1]).astype(BF16)

    arrived(0, a_r.at[0:15])
    s1 = [(a_r[2 * m].astype(F32) + a_r[2 * m + 1].astype(F32)).astype(BF16) for m in range(8)]
    s1p = [jnp.concatenate(s1[2 * m:2 * m + 2], axis=1) for m in range(4)]
    root_v[...] = mm(jnp.concatenate(s1, axis=1), u_v[...]).astype(BF16)

    for j in grp_peers:
        remote(2, "grp", root_v, b_r.at[g], j).start()
    b_r[g] = root_v[...]

    s2 = [mm(s1p[m], iop_v[0, 2 * m:2 * m + 2].reshape(2 * R, R)).astype(BF16) for m in range(4)]
    s2p = [jnp.concatenate(s2[2 * m:2 * m + 2], axis=1) for m in range(2)]
    s3 = [mm(s2p[m], iop_v[0, 8 + 2 * m:10 + 2 * m].reshape(2 * R, R)).astype(BF16) for m in range(2)]
    c3 = [mmt(s3[1 - m], iop_v[2, 12 + m]).astype(BF16) for m in range(2)]
    c2 = [(mmt(s2[m ^ 1], iop_v[2, 8 + m]) + mmt(c3[m // 2], iop_v[1, 8 + m])).astype(BF16) for m in range(4)]
    c1 = [mmt(s1[m ^ 1], iop_v[2, m]) + mmt(c2[m // 2], iop_v[1, m]) for m in range(8)]
    l_diag.wait()
    ridge = ridge_s[0]
    for t in range(3):
        rows = pl.ds(t * 512, 512)
        loc_v[rows, :] = mm(diag_v[rows, :], og_v[...]) + ridge * og_v[rows, :].astype(F32)
    arrived(1, sib_v)
    near = mmt(sib_v[...], lop_v[2]).astype(BF16)
    loc_v[...] = loc_v[...] + mmt(dn_v[...], near)

    arrived(2, b_r.at[0:15])
    c4 = mm(jnp.concatenate([b_r[j] for j in range(D)], axis=1), t_v[...].reshape(D * R, R)).astype(BF16)
    down = mmt(c4, q_v[...])
    for m in range(8):
        c_v[m] = (c1[m] + down[:, m * R:(m + 1) * R]).astype(BF16)

    for j in z_peers:
        remote(3, "leaf", c_v.at[j // 2], c_r.at[z, core], j).start()
    c_r[z, core] = c_v[z]

    xt_v[:K, :] = og_v[...].T
    l_res.wait()
    for t in range(3):
        rows = pl.ds(t * 512, 512)
        xt_v[K:, rows] = mm(p_v[rows, :], res_v[...]).astype(BF16).T
    im_v[...] = loc_v[...].astype(BF16)
    for t in range(2):
        pre_v[t] = mm(xt_v[t * K:(t + 1) * K, :], im_v[...])
    xv_v[...] = mm(xt_v[...], vr_v[...]).astype(BF16).reshape(2, K, R)

    arrived(3, c_v.at[0:7])
    remote(4, "leaf", c_r.at[:, core], c_r.at[:, core], sibling).start()
    arrived(4, c_v)

    coarse = c_r[...].reshape(K, R)
    gs_v[...] = (pre_v[1 - core] + mmt(xv_v[1 - core], coarse)).astype(BF16)
    remote(5, "leaf", gs_v, gs_r, sibling).start()
    own = pre_v[core] + mmt(xv_v[core], coarse)
    im_v[...] = (loc_v[...] + mmt(vr_v[...], coarse)).astype(BF16)
    arrived(5, gs_r)
    h_v[...] = (own + gs_r[...].astype(F32)).astype(BF16).reshape(D, C, K)
    for j in grp_peers:
        remote(6, "grp", h_v.at[j], h_r.at[g], j).start()
    h_r[g] = h_v[g]

    for t in range(3):
        rows = pl.ds(t * 512, 512)
        img_v[rows, :] = mm(pt_v[rows, :], im_v[...]).astype(BF16)

    arrived(6, h_r.at[0:15])
    total = h_r[0].astype(F32)
    for j in range(1, D):
        total = total + h_r[j].astype(F32)
    z_v[...] = total.astype(BF16)
    for j in z_peers:
        remote(7, "leaf", z_v, z_r.at[z], j).start()
    z_r[z] = z_v[...]
    arrived(7, z_r.at[0:7])
    total = z_r[0].astype(F32)
    for j in range(1, D // 2):
        total = total + z_r[j].astype(F32)
    f_v[...] = total.astype(BF16)
    for j in grp_peers:
        remote(8, "grp", f_v, f_r.at[g], j).start()
    f_r[g] = f_v[...]
    arrived(8, f_r.at[0:15])
    remote(9, "leaf", f_r, o_r, sibling).start()
    scale = 1.0 / (N * D * D)
    out_v[core] = f_r[...].reshape(K, K).astype(F32) * scale
    arrived(9, o_r)
    out_v[1 - core] = o_r[...].reshape(K, K).astype(F32) * scale
    for phase, ref in enumerate((
        l1_v.at[0:15], s0_v, b_r.at[0:15], c_v.at[0:7], c_v, gs_v, h_v.at[0:15], z_r.at[0:7], f_r.at[0:15], f_r,
    )):
        left(phase, ref)


def finish(image, grams, img_h, cur_h, cor_h, sem):
    rows = [pl.ds(t * 256, 256) for t in range(N // 256)]
    pairs = [(image.at[r], img_h.at[r]) for r in rows]
    pairs += [(grams.at[i, pl.ds(t * 128, 128)], dst.at[pl.ds(t * 128, 128)]) for i, dst in enumerate((cur_h, cor_h)) for t in range(2)]
    copies = [pltpu.make_async_copy(src, dst, sem.at[i]) for i, (src, dst) in enumerate(pairs)]
    for copy in copies:
        copy.start()
    for copy in copies:
        copy.wait()


def body(*args):
    any_spec = pl.BlockSpec(memory_space=pl.ANY)
    vmem_spec = pl.BlockSpec(memory_space=pltpu.VMEM)
    dma = pltpu.SemaphoreType.DMA
    v = pltpu.VMEM
    scratch = [
        v((N, K), BF16), v((N, K), BF16), v((1, N), jnp.int32), v((N, N), BF16), v((N, R), BF16), v((N, R), BF16),
        v((3, R, R), BF16), v((3, 14, R, R), BF16), v((28, R, R), BF16), v((7, R, R), BF16),
        v((N, N), BF16), v((N, N), BF16), v((N, K), BF16), v((2 * K, N), BF16), v((N, K), F32), v((N, K), BF16),
        v((K, R), BF16), v((K, R), BF16), v((D, C, R), BF16), v((D, C, R), BF16), v((C, R), BF16), v((D, C, R), BF16),
        v((D, R, R), BF16), v((8 * R, R), BF16), v((8 * R, R), BF16), v((N, R), BF16), v((2, K, R), BF16), v((8, C, R), BF16), v((8, 2, C, R), BF16),
        v((2, K, K), F32), v((K, K), BF16), v((K, K), BF16), v((D, C, K), BF16), v((D, C, K), BF16), v((C, K), BF16),
        v((8, C, K), BF16), v((C, K), BF16), v((D, C, K), BF16), v((D, C, K), BF16),
        dma((10,)), dma((10,)), dma((10,)),
    ]
    args = [pltpu.with_memory_space_constraint(a, pltpu.HBM) for a in args[:-1]] + [args[-1]]
    image, grams = pl.pallas_call(
        kernel,
        out_shape=(jax.ShapeDtypeStruct((N, K), BF16), jax.ShapeDtypeStruct((2, K, K), F32)),
        in_specs=[any_spec] * 9 + [pl.BlockSpec(memory_space=pltpu.SMEM)],
        out_specs=(vmem_spec, vmem_spec),
        scratch_shapes=scratch,
        compiler_params=pltpu.CompilerParams(
            collective_id=0, has_side_effects=True, vmem_limit_bytes=48 * 1024 * 1024),
    )(*args)
    return pl.pallas_call(
        finish,
        out_shape=(jax.ShapeDtypeStruct((N, K), BF16), jax.ShapeDtypeStruct((K, K), F32), jax.ShapeDtypeStruct((K, K), F32)),
        in_specs=[any_spec, any_spec],
        out_specs=(any_spec, any_spec, any_spec),
        scratch_shapes=[dma((10,))],
        compiler_params=pltpu.CompilerParams(vmem_limit_bytes=1024 * 1024),
    )(image, grams)


def solution(mesh):
    in_specs = (
        P(GRP_LEAF, None), P(GRP_LEAF, None), P(GRP_LEAF, None), P(GRP_LEAF, None, None), P(GRP_LEAF, None, None),
        P(GRP_LEAF, None, None), P(None, GRP_LEAF, None, None), P(None, "grp", None, None), P(), P(),
    )
    return jax.shard_map(
        body, mesh=mesh, in_specs=in_specs, out_specs=(P(GRP_LEAF, None), P(), P()), check_vma=False)
```

```python
import jax
import jax.numpy as jnp
from jax import lax
from jax.experimental import pallas as pl
from jax.experimental.pallas import tpu as pltpu
from jax.sharding import PartitionSpec as P

F32 = jnp.float32
BF16 = jnp.bfloat16
GRP_LEAF = ("grp", "leaf")
N = 1536
R = 128
K = 256
D = 16
C = K // D


def mm(a, b):
    return lax.dot_general(a, b, (((1,), (0,)), ((), ())), preferred_element_type=F32)


def mmt(a, b):
    return lax.dot_general(a, b, (((1,), (1,)), ((), ())), preferred_element_type=F32)


def kernel(
    x_h, res_h, ord_h, diag_h, up_h, dn_h, lop_h, iop_h, top_h, ridge_s,
    img_v, out_v,
    x_v, res_v, ord_v, diag_v, up_v, dn_v, lop_v, iop_v, w_v, path_v,
    p_v, pt_v, og_v, xt_v, loc_v, im_v,
    s0_v, sib_v, l1_v, a_r, root_v, b_r, t_v, u_v, q_v, vr_v, xv_v, c_v, c_r,
    pre_v, ps_v, ps_r, po_v, xs_v, xs_r, h_v, h_r, z_v, z_r, f_v, f_r, o_r,
    load_sem, send_sem, recv_sem,
):
    me = lax.axis_index("leaf")
    g = lax.axis_index("grp")
    core = lax.rem(me, 2)
    z = me // 2
    sibling = me + 1 - 2 * core

    leaf_peers = [lax.rem(me + r, D) for r in sorted(range(1, D), key=lambda r: -min(r, D - r))]
    z_peers = [lax.rem(me + 2 * r, D) for r in sorted(range(1, D // 2), key=lambda r: -min(r, D // 2 - r))]
    steps = sorted(((dy, dx) for dy in range(4) for dx in range(4) if dy or dx),
                   key=lambda s: -(min(s[0], 4 - s[0]) + min(s[1], 4 - s[1])))
    gy, gx = g // 4, lax.rem(g, 4)
    grp_peers = [lax.rem(gy + dy, 4) * 4 + lax.rem(gx + dx, 4) for dy, dx in steps]

    def block_of(j):
        return lax.rem(j, 2) * (D // 2) + j // 2

    own_half = pl.ds(pl.multiple_of(core * R, R), R)
    other_half = pl.ds(pl.multiple_of((1 - core) * R, R), R)

    def sib_of(a):
        return a + 1 - 2 * lax.rem(a, 2)

    def remote(phase, axis, src, dst, j):
        return pltpu.make_async_remote_copy(
            src_ref=src, dst_ref=dst, send_sem=send_sem.at[phase], recv_sem=recv_sem.at[phase],
            device_id={axis: j}, device_id_type=pl.DeviceIdType.MESH)

    def arrived(phase, ref):
        remote(phase, "leaf", ref, ref, sibling).wait_recv()

    def left(phase, ref):
        remote(phase, "leaf", ref, ref, sibling).wait_send()

    a4, a5, a6, a7 = g, g // 2, g // 4, g // 8
    def start_all(copies):
        for copy in copies:
            copy.start()

    def load(slot, src, dst):
        return pltpu.make_async_copy(src, dst, load_sem.at[slot])

    l_ord = load(0, ord_h, ord_v)
    l_up = load(1, up_h.at[0], up_v)
    l_lop = load(2, lop_h.at[:, 0], lop_v)
    l_x = load(3, x_h, x_v)
    start_all([l_ord, l_up, l_lop, l_x])
    l_iop = load(4, iop_h, iop_v)
    l_lift = load(5, top_h.at[0, 0:28], w_v)
    path = [(1, a4), (1, 16 + a5), (1, 24 + a6), (2, a4), (2, 16 + a5), (2, 24 + a6), (2, 28 + a7)]
    l_path = [load(6, top_h.at[kind, node], path_v.at[i]) for i, (kind, node) in enumerate(path)]
    l_dn = load(7, dn_h.at[0], dn_v)
    l_diag = load(8, diag_h.at[0], diag_v)
    l_res = load(9, res_h, res_v)

    barrier = pltpu.get_barrier_semaphore()
    for j in leaf_peers:
        pl.semaphore_signal(barrier, inc=1, device_id={"leaf": j}, device_id_type=pl.DeviceIdType.MESH)
    for j in grp_peers:
        pl.semaphore_signal(barrier, inc=1, device_id={"grp": j}, device_id_type=pl.DeviceIdType.MESH)

    l_ord.wait()
    order = ord_v[...]
    column = jnp.broadcast_to(order.astype(F32), (R, N)).T.astype(jnp.int32)
    lane = lax.broadcasted_iota(jnp.int32, (N, R), 1)
    low = jnp.where((column & (R - 1)) == lane, 1.0, 0.0).astype(BF16)
    high = (column >> 7).astype(BF16)
    for j in range(N // R):
        p_v[:, j * R:(j + 1) * R] = jnp.where(high == jnp.asarray(j, BF16), low, jnp.zeros_like(low))

    l_up.wait()
    l_lop.wait()
    up_t = up_v[...].T
    lift_t = lax.dot_general(lop_v[0], up_t, (((0,), (0,)), ((), ())), preferred_element_type=F32).astype(BF16)
    both_t = jnp.concatenate([up_t, lift_t], axis=0)

    both_t = mm(both_t, p_v[...]).astype(BF16)
    l_x.wait()
    start_all([l_iop, l_lift, *l_path, l_dn, l_diag, l_res])
    both = mm(both_t, x_v[...]).T
    s0_v[...] = both[:, :R].astype(BF16)
    l1_v[...] = both[:, R:].astype(BF16).reshape(D, C, R)

    pl.semaphore_wait(barrier, 2 * (D - 1))

    for j in leaf_peers:
        remote(0, "leaf", l1_v.at[block_of(j)], a_r.at[me], j).start()
    remote(1, "leaf", s0_v, sib_v, sibling).start()
    a_r[me] = l1_v[block_of(me)]

    for t in range(3):
        rows = pl.ds(t * 512, 512)
        og_v[rows, :] = mm(p_v[rows, :], x_v[...]).astype(BF16)
    l_iop.wait()
    up2 = [mm(iop_v[0, 8 + 2 * m:10 + 2 * m].reshape(2 * R, R), iop_v[0, 12 + m]).astype(BF16) for m in range(2)]
    for m in range(4):
        u_v[2 * R * m:2 * R * (m + 1), :] = mm(
            iop_v[0, 2 * m:2 * m + 2].reshape(2 * R, R), up2[m // 2][(m % 2) * R:(m % 2 + 1) * R]).astype(BF16)
    q2 = [mm(iop_v[1, 8 + m], iop_v[1, 12 + m // 2]).astype(BF16) for m in range(4)]
    for m in range(8):
        q_v[m * R:(m + 1) * R, :] = mm(iop_v[1, m], q2[m // 2]).astype(BF16)
    l_lift.wait()
    load(6, top_h.at[1, 0:7], path_v).wait()
    y5 = path_v[0]
    y6 = mm(y5, path_v[1]).astype(BF16)
    y7 = mm(y6, path_v[2]).astype(BF16)
    x5 = mm(y5, path_v[4]).astype(BF16)
    x6 = mm(y6, path_v[5]).astype(BF16)
    x7 = mm(y7, path_v[6]).astype(BF16)

    def lifts(base, node, count):
        return w_v[pl.ds(base + node, count)].reshape(count * R, R)

    t_v[g] = jnp.zeros((R, R), BF16)
    n4, n5, n6, n7 = sib_of(a4), sib_of(a5), sib_of(a6), sib_of(a7)
    t_v[n4] = path_v[3].T
    t_v[pl.ds(2 * n5, 2)] = mmt(lifts(0, 2 * n5, 2), x5).astype(BF16).reshape(2, R, R)
    w = mmt(lifts(16, 2 * n6, 2), x6).astype(BF16)
    for b in range(2):
        t_v[pl.ds(4 * n6 + 2 * b, 2)] = mm(lifts(0, 4 * n6 + 2 * b, 2), w[b * R:(b + 1) * R]).astype(BF16).reshape(2, R, R)
    w = mmt(lifts(24, 2 * n7, 2), x7).astype(BF16)
    for b in range(2):
        u = mm(lifts(16, 4 * n7 + 2 * b, 2), w[b * R:(b + 1) * R]).astype(BF16)
        for d in range(2):
            first = 8 * n7 + 4 * b + 2 * d
            t_v[pl.ds(first, 2)] = mm(lifts(0, first, 2), u[d * R:(d + 1) * R]).astype(BF16).reshape(2, R, R)

    row_low = jnp.broadcast_to(order & (R - 1), (R, N))
    row_high = jnp.broadcast_to(order >> 7, (R, N)).astype(F32).astype(BF16)
    row_one = jnp.where(row_low == lax.broadcasted_iota(jnp.int32, (R, N), 0), 1.0, 0.0).astype(BF16)
    for j in range(N // R):
        pt_v[j * R:(j + 1) * R, :] = jnp.where(row_high == jnp.asarray(j, BF16), row_one, jnp.zeros_like(row_one))
    l_dn.wait()
    vr_v[...] = mm(dn_v[...], lop_v[1]).astype(BF16)
    xt_v[:K, :] = og_v[...].T

    arrived(0, a_r.at[0:15])
    s1 = [(a_r[2 * m].astype(F32) + a_r[2 * m + 1].astype(F32)).astype(BF16) for m in range(8)]
    s1p = [jnp.concatenate(s1[2 * m:2 * m + 2], axis=1) for m in range(4)]
    root_v[...] = mm(jnp.concatenate(s1, axis=1), u_v[...]).astype(BF16)

    for j in grp_peers:
        remote(2, "grp", root_v, b_r.at[g], j).start()
    b_r[g] = root_v[...]

    s2 = [mm(s1p[m], iop_v[0, 2 * m:2 * m + 2].reshape(2 * R, R)).astype(BF16) for m in range(4)]
    s2p = [jnp.concatenate(s2[2 * m:2 * m + 2], axis=1) for m in range(2)]
    s3 = [mm(s2p[m], iop_v[0, 8 + 2 * m:10 + 2 * m].reshape(2 * R, R)).astype(BF16) for m in range(2)]
    c3 = [mmt(s3[1 - m], iop_v[2, 12 + m]).astype(BF16) for m in range(2)]
    c2 = [(mmt(s2[m ^ 1], iop_v[2, 8 + m]) + mmt(c3[m // 2], iop_v[1, 8 + m])).astype(BF16) for m in range(4)]
    c1 = [mmt(s1[m ^ 1], iop_v[2, m]) + mmt(c2[m // 2], iop_v[1, m]) for m in range(8)]
    l_diag.wait()
    ridge = ridge_s[0]
    for t in range(3):
        rows = pl.ds(t * 512, 512)
        loc_v[rows, :] = mm(diag_v[rows, :], og_v[...]) + ridge * og_v[rows, :].astype(F32)
    arrived(1, sib_v)
    near = mmt(sib_v[...], lop_v[2]).astype(BF16)
    loc_v[...] = loc_v[...] + mmt(dn_v[...], near)
    l_res.wait()
    for t in range(3):
        rows = pl.ds(t * 512, 512)
        xt_v[K:, rows] = mm(p_v[rows, :], res_v[...]).astype(BF16).T

    arrived(2, b_r.at[0:15])
    c4 = mm(jnp.concatenate([b_r[j] for j in range(D)], axis=1), t_v[...].reshape(D * R, R)).astype(BF16)
    down = mmt(c4, q_v[...])
    for m in range(8):
        c_v[m] = (c1[m] + down[:, m * R:(m + 1) * R]).astype(BF16)

    for j in z_peers:
        remote(3, "leaf", c_v.at[j // 2], c_r.at[core, z], j).start()
    c_r[core, z] = c_v[z]

    im_v[...] = loc_v[...].astype(BF16)
    xv_v[...] = mm(xt_v[...], vr_v[...]).astype(BF16)
    remote(10, "leaf", xv_v, xs_r, sibling).start()
    for t in range(2):
        rows = pl.ds(t * K, K)
        pre_v[rows, :] = mm(xt_v[rows, :], im_v[...])
    ps_v[...] = pre_v[:, other_half].astype(BF16)
    remote(5, "leaf", ps_v, ps_r, sibling).start()
    arrived(10, xs_r)
    xs_v[...] = (xv_v[...].astype(F32) + xs_r[...].astype(F32)).astype(BF16)
    arrived(5, ps_r)
    po_v[...] = pre_v[:, own_half] + ps_r[...].astype(F32)

    arrived(3, c_v.at[0:7])
    remote(4, "leaf", c_r.at[core], c_r.at[core], sibling).start()

    h_v[...] = (po_v[...] + mmt(xs_v[...], c_r[core].reshape(R, R))).astype(BF16).reshape(D, 2 * C, R)
    for j in grp_peers:
        remote(6, "grp", h_v.at[j], h_r.at[g], j).start()
    h_r[g] = h_v[g]

    arrived(4, c_v)
    im_v[...] = (loc_v[...] + mmt(vr_v[...], c_r[...].reshape(K, R))).astype(BF16)
    for t in range(3):
        rows = pl.ds(t * 512, 512)
        img_v[rows, :] = mm(pt_v[rows, :], im_v[...]).astype(BF16)

    arrived(6, h_r.at[0:15])
    total = h_r[0].astype(F32)
    for j in range(1, D):
        total = total + h_r[j].astype(F32)
    z_v[...] = total.astype(BF16)
    for j in z_peers:
        remote(7, "leaf", z_v, z_r.at[z], j).start()
    z_r[z] = z_v[...]
    arrived(7, z_r.at[0:7])
    total = z_r[0].astype(F32)
    for j in range(1, D // 2):
        total = total + z_r[j].astype(F32)
    f_v[...] = total.astype(BF16)
    for j in grp_peers:
        remote(8, "grp", f_v, f_r.at[g], j).start()
    f_r[g] = f_v[...]
    arrived(8, f_r.at[0:15])
    remote(9, "leaf", f_r, o_r, sibling).start()
    scale = 1.0 / (N * D * D)
    out_v[:, :, own_half] = (f_r[...].astype(F32) * scale).reshape(2, K, R)
    arrived(9, o_r)
    out_v[:, :, other_half] = (o_r[...].astype(F32) * scale).reshape(2, K, R)
    for phase, ref in enumerate((
        l1_v.at[0:15], s0_v, b_r.at[0:15], c_v.at[0:7], c_v, ps_v, h_v.at[0:15], z_r.at[0:7], f_r.at[0:15], f_r, xv_v,
    )):
        left(phase, ref)


def finish(image, grams, img_h, cur_h, cor_h, sem):
    rows = [pl.ds(t * 256, 256) for t in range(N // 256)]
    pairs = [(image.at[r], img_h.at[r]) for r in rows]
    pairs += [(grams.at[i, pl.ds(t * 128, 128)], dst.at[pl.ds(t * 128, 128)]) for i, dst in enumerate((cur_h, cor_h)) for t in range(2)]
    copies = [pltpu.make_async_copy(src, dst, sem.at[i]) for i, (src, dst) in enumerate(pairs)]
    for copy in copies:
        copy.start()
    for copy in copies:
        copy.wait()


def body(*args):
    any_spec = pl.BlockSpec(memory_space=pl.ANY)
    vmem_spec = pl.BlockSpec(memory_space=pltpu.VMEM)
    dma = pltpu.SemaphoreType.DMA
    v = pltpu.VMEM
    scratch = [
        v((N, K), BF16), v((N, K), BF16), v((1, N), jnp.int32), v((N, N), BF16), v((N, R), BF16), v((N, R), BF16),
        v((3, R, R), BF16), v((3, 14, R, R), BF16), v((28, R, R), BF16), v((7, R, R), BF16),
        v((N, N), BF16), v((N, N), BF16), v((N, K), BF16), v((2 * K, N), BF16), v((N, K), F32), v((N, K), BF16),
        v((K, R), BF16), v((K, R), BF16), v((D, C, R), BF16), v((D, C, R), BF16), v((C, R), BF16), v((D, C, R), BF16),
        v((D, R, R), BF16), v((8 * R, R), BF16), v((8 * R, R), BF16), v((N, R), BF16), v((2 * K, R), BF16), v((8, C, R), BF16), v((2, 8, C, R), BF16),
        v((2 * K, K), F32), v((2 * K, R), BF16), v((2 * K, R), BF16), v((2 * K, R), F32), v((2 * K, R), BF16), v((2 * K, R), BF16),
        v((D, 2 * C, R), BF16), v((D, 2 * C, R), BF16), v((2 * C, R), BF16), v((8, 2 * C, R), BF16), v((2 * C, R), BF16),
        v((D, 2 * C, R), BF16), v((D, 2 * C, R), BF16),
        dma((10,)), dma((11,)), dma((11,)),
    ]
    args = [pltpu.with_memory_space_constraint(a, pltpu.HBM) for a in args[:-1]] + [args[-1]]
    image, grams = pl.pallas_call(
        kernel,
        out_shape=(jax.ShapeDtypeStruct((N, K), BF16), jax.ShapeDtypeStruct((2, K, K), F32)),
        in_specs=[any_spec] * 9 + [pl.BlockSpec(memory_space=pltpu.SMEM)],
        out_specs=(vmem_spec, vmem_spec),
        scratch_shapes=scratch,
        compiler_params=pltpu.CompilerParams(
            collective_id=0, has_side_effects=True, vmem_limit_bytes=48 * 1024 * 1024),
    )(*args)
    return pl.pallas_call(
        finish,
        out_shape=(jax.ShapeDtypeStruct((N, K), BF16), jax.ShapeDtypeStruct((K, K), F32), jax.ShapeDtypeStruct((K, K), F32)),
        in_specs=[any_spec, any_spec],
        out_specs=(any_spec, any_spec, any_spec),
        scratch_shapes=[dma((10,))],
        compiler_params=pltpu.CompilerParams(vmem_limit_bytes=1024 * 1024),
    )(image, grams)


def solution(mesh):
    in_specs = (
        P(GRP_LEAF, None), P(GRP_LEAF, None), P(GRP_LEAF, None), P(GRP_LEAF, None, None), P(GRP_LEAF, None, None),
        P(GRP_LEAF, None, None), P(None, GRP_LEAF, None, None), P(None, "grp", None, None), P(), P(),
    )
    return jax.shard_map(
        body, mesh=mesh, in_specs=in_specs, out_specs=(P(GRP_LEAF, None), P(), P()), check_vma=False)
```

```python
import jax
import jax.numpy as jnp
from jax import lax
from jax.experimental import pallas as pl
from jax.experimental.pallas import tpu as pltpu
from jax.sharding import PartitionSpec as P

F32 = jnp.float32
BF16 = jnp.bfloat16
GRP_LEAF = ("grp", "leaf")
N = 1536
R = 128
K = 256
D = 16
C = K // D


def mm(a, b):
    return lax.dot_general(a, b, (((1,), (0,)), ((), ())), preferred_element_type=F32)


def mmt(a, b):
    return lax.dot_general(a, b, (((1,), (1,)), ((), ())), preferred_element_type=F32)


def kernel(
    x_h, res_h, ord_h, diag_h, up_h, dn_h, lop_h, iop_h, top_h, ridge_s,
    img_v, out_v,
    x_v, res_v, ord_v, diag_v, up_v, dn_v, lop_v, iop_v, w_v, path_v,
    p_v, pt_v, og_v, xt_v, loc_v, im_v,
    s0_v, sib_v, l1_v, a_r, root_v, b_r, t_v, u_v, q_v, vr_v, xv_v, c_v, c_r,
    pre_v, ps_v, ps_r, po_v, xs_v, xs_r, h_v, h_r, z_v, z_r, f_v, f_r, o_r,
    load_sem, send_sem, recv_sem,
):
    me = lax.axis_index("leaf")
    g = lax.axis_index("grp")
    core = lax.rem(me, 2)
    z = me // 2
    sibling = me + 1 - 2 * core

    leaf_peers = [lax.rem(me + r, D) for r in sorted(range(1, D), key=lambda r: -min(r, D - r))]
    z_peers = [lax.rem(me + 2 * r, D) for r in sorted(range(1, D // 2), key=lambda r: -min(r, D // 2 - r))]
    steps = sorted(((dy, dx) for dy in range(4) for dx in range(4) if dy or dx),
                   key=lambda s: -(min(s[0], 4 - s[0]) + min(s[1], 4 - s[1])))
    gy, gx = g // 4, lax.rem(g, 4)
    grp_peers = [lax.rem(gy + dy, 4) * 4 + lax.rem(gx + dx, 4) for dy, dx in steps]

    def block_of(j):
        return lax.rem(j, 2) * (D // 2) + j // 2

    own_half = pl.ds(pl.multiple_of(core * R, R), R)
    other_half = pl.ds(pl.multiple_of((1 - core) * R, R), R)

    def sib_of(a):
        return a + 1 - 2 * lax.rem(a, 2)

    def remote(phase, axis, src, dst, j):
        return pltpu.make_async_remote_copy(
            src_ref=src, dst_ref=dst, send_sem=send_sem.at[phase], recv_sem=recv_sem.at[phase],
            device_id={axis: j}, device_id_type=pl.DeviceIdType.MESH)

    def arrived(phase, ref):
        remote(phase, "leaf", ref, ref, sibling).wait_recv()

    def left(phase, ref):
        remote(phase, "leaf", ref, ref, sibling).wait_send()

    a4, a5, a6, a7 = g, g // 2, g // 4, g // 8
    def start_all(copies):
        for copy in copies:
            copy.start()

    def load(slot, src, dst):
        return pltpu.make_async_copy(src, dst, load_sem.at[slot])

    l_ord = load(0, ord_h, ord_v)
    l_up = load(1, up_h.at[0], up_v)
    l_lop = load(2, lop_h.at[:, 0], lop_v)
    l_x = load(3, x_h, x_v)
    start_all([l_ord, l_up, l_lop, l_x])
    l_iop = load(4, iop_h, iop_v)
    l_lift = load(5, top_h.at[0, 0:28], w_v)
    path = [(1, a4), (1, 16 + a5), (1, 24 + a6), (2, a4), (2, 16 + a5), (2, 24 + a6), (2, 28 + a7)]
    l_path = [load(6, top_h.at[kind, node], path_v.at[i]) for i, (kind, node) in enumerate(path)]
    l_dn = load(7, dn_h.at[0], dn_v)
    l_diag = load(8, diag_h.at[0], diag_v)
    l_res = load(9, res_h, res_v)

    barrier = pltpu.get_barrier_semaphore()
    for j in leaf_peers:
        pl.semaphore_signal(barrier, inc=1, device_id={"leaf": j}, device_id_type=pl.DeviceIdType.MESH)
    for j in grp_peers:
        pl.semaphore_signal(barrier, inc=1, device_id={"grp": j}, device_id_type=pl.DeviceIdType.MESH)

    l_ord.wait()
    order = ord_v[...]
    column = jnp.broadcast_to(order.astype(F32), (R, N)).T.astype(jnp.int32)
    lane = lax.broadcasted_iota(jnp.int32, (N, R), 1)
    low = jnp.where((column & (R - 1)) == lane, 1.0, 0.0).astype(BF16)
    high = (column >> 7).astype(BF16)
    for j in range(N // R):
        p_v[:, j * R:(j + 1) * R] = jnp.where(high == jnp.asarray(j, BF16), low, jnp.zeros_like(low))

    l_up.wait()
    l_lop.wait()
    up_t = up_v[...].T
    lift_t = lax.dot_general(lop_v[0], up_t, (((0,), (0,)), ((), ())), preferred_element_type=F32).astype(BF16)
    both_t = jnp.concatenate([up_t, lift_t], axis=0)

    both_t = mm(both_t, p_v[...]).astype(BF16)
    l_x.wait()
    start_all([l_iop, l_lift, *l_path, l_dn, l_diag, l_res])
    both = mm(both_t, x_v[...]).T
    s0_v[...] = both[:, :R].astype(BF16)
    l1_v[...] = both[:, R:].astype(BF16).reshape(D, C, R)

    pl.semaphore_wait(barrier, 2 * (D - 1))

    for j in leaf_peers:
        remote(0, "leaf", l1_v.at[block_of(j)], a_r.at[me], j).start()
    remote(1, "leaf", s0_v, sib_v, sibling).start()
    a_r[me] = l1_v[block_of(me)]

    for t in range(3):
        rows = pl.ds(t * 512, 512)
        og_v[rows, :] = mm(p_v[rows, :], x_v[...]).astype(BF16)
    l_iop.wait()
    up2 = [mm(iop_v[0, 8 + 2 * m:10 + 2 * m].reshape(2 * R, R), iop_v[0, 12 + m]).astype(BF16) for m in range(2)]
    for m in range(4):
        u_v[2 * R * m:2 * R * (m + 1), :] = mm(
            iop_v[0, 2 * m:2 * m + 2].reshape(2 * R, R), up2[m // 2][(m % 2) * R:(m % 2 + 1) * R]).astype(BF16)
    q2 = [mm(iop_v[1, 8 + m], iop_v[1, 12 + m // 2]).astype(BF16) for m in range(4)]
    for m in range(8):
        q_v[m * R:(m + 1) * R, :] = mm(iop_v[1, m], q2[m // 2]).astype(BF16)
    l_lift.wait()
    load(6, top_h.at[1, 0:7], path_v).wait()
    y5 = path_v[0]
    y6 = mm(y5, path_v[1]).astype(BF16)
    y7 = mm(y6, path_v[2]).astype(BF16)
    x5 = mm(y5, path_v[4]).astype(BF16)
    x6 = mm(y6, path_v[5]).astype(BF16)
    x7 = mm(y7, path_v[6]).astype(BF16)

    def lifts(base, node, count):
        return w_v[pl.ds(base + node, count)].reshape(count * R, R)

    t_v[g] = jnp.zeros((R, R), BF16)
    n4, n5, n6, n7 = sib_of(a4), sib_of(a5), sib_of(a6), sib_of(a7)
    t_v[n4] = path_v[3].T
    t_v[pl.ds(2 * n5, 2)] = mmt(lifts(0, 2 * n5, 2), x5).astype(BF16).reshape(2, R, R)
    w = mmt(lifts(16, 2 * n6, 2), x6).astype(BF16)
    for b in range(2):
        t_v[pl.ds(4 * n6 + 2 * b, 2)] = mm(lifts(0, 4 * n6 + 2 * b, 2), w[b * R:(b + 1) * R]).astype(BF16).reshape(2, R, R)
    w = mmt(lifts(24, 2 * n7, 2), x7).astype(BF16)
    for b in range(2):
        u = mm(lifts(16, 4 * n7 + 2 * b, 2), w[b * R:(b + 1) * R]).astype(BF16)
        for d in range(2):
            first = 8 * n7 + 4 * b + 2 * d
            t_v[pl.ds(first, 2)] = mm(lifts(0, first, 2), u[d * R:(d + 1) * R]).astype(BF16).reshape(2, R, R)

    row_low = jnp.broadcast_to(order & (R - 1), (R, N))
    row_high = jnp.broadcast_to(order >> 7, (R, N)).astype(F32).astype(BF16)
    row_one = jnp.where(row_low == lax.broadcasted_iota(jnp.int32, (R, N), 0), 1.0, 0.0).astype(BF16)
    for j in range(N // R):
        pt_v[j * R:(j + 1) * R, :] = jnp.where(row_high == jnp.asarray(j, BF16), row_one, jnp.zeros_like(row_one))
    l_dn.wait()
    vr_v[...] = mm(dn_v[...], lop_v[1]).astype(BF16)
    xt_v[:K, :] = og_v[...].T

    arrived(0, a_r.at[0:15])
    s1 = [(a_r[2 * m].astype(F32) + a_r[2 * m + 1].astype(F32)).astype(BF16) for m in range(8)]
    s1p = [jnp.concatenate(s1[2 * m:2 * m + 2], axis=1) for m in range(4)]
    root_v[...] = mm(jnp.concatenate(s1, axis=1), u_v[...]).astype(BF16)

    for j in grp_peers:
        remote(2, "grp", root_v, b_r.at[g], j).start()
    b_r[g] = root_v[...]

    s2 = [mm(s1p[m], iop_v[0, 2 * m:2 * m + 2].reshape(2 * R, R)).astype(BF16) for m in range(4)]
    s2p = [jnp.concatenate(s2[2 * m:2 * m + 2], axis=1) for m in range(2)]
    s3 = [mm(s2p[m], iop_v[0, 8 + 2 * m:10 + 2 * m].reshape(2 * R, R)).astype(BF16) for m in range(2)]
    c3 = [mmt(s3[1 - m], iop_v[2, 12 + m]).astype(BF16) for m in range(2)]
    c2 = [(mmt(s2[m ^ 1], iop_v[2, 8 + m]) + mmt(c3[m // 2], iop_v[1, 8 + m])).astype(BF16) for m in range(4)]
    c1 = [mmt(s1[m ^ 1], iop_v[2, m]) + mmt(c2[m // 2], iop_v[1, m]) for m in range(8)]
    l_diag.wait()
    ridge = ridge_s[0]
    for t in range(3):
        rows = pl.ds(t * 512, 512)
        loc_v[rows, :] = mm(diag_v[rows, :], og_v[...]) + ridge * og_v[rows, :].astype(F32)
    arrived(1, sib_v)
    near = mmt(sib_v[...], lop_v[2]).astype(BF16)
    loc_v[...] = loc_v[...] + mmt(dn_v[...], near)
    l_res.wait()
    for t in range(3):
        rows = pl.ds(t * 512, 512)
        xt_v[K:, rows] = mm(p_v[rows, :], res_v[...]).astype(BF16).T

    arrived(2, b_r.at[0:15])
    c4 = mm(jnp.concatenate([b_r[j] for j in range(D)], axis=1), t_v[...].reshape(D * R, R)).astype(BF16)
    down = mmt(c4, q_v[...])
    for m in range(8):
        c_v[m] = (c1[m] + down[:, m * R:(m + 1) * R]).astype(BF16)

    for j in z_peers:
        remote(3, "leaf", c_v.at[j // 2], c_r.at[core, z], j).start()
    c_r[core, z] = c_v[z]

    im_v[...] = loc_v[...].astype(BF16)
    xv_v[...] = mm(xt_v[...], vr_v[...]).astype(BF16)
    remote(10, "leaf", xv_v, xs_r, sibling).start()
    for t in range(2):
        rows = pl.ds(t * K, K)
        pre_v[rows, :] = mm(xt_v[rows, :], im_v[...])
    ps_v[...] = pre_v[:, other_half].astype(BF16)
    remote(5, "leaf", ps_v, ps_r, sibling).start()
    arrived(10, xs_r)
    xs_v[...] = (xv_v[...].astype(F32) + xs_r[...].astype(F32)).astype(BF16)
    arrived(5, ps_r)
    po_v[...] = pre_v[:, own_half] + ps_r[...].astype(F32)

    arrived(3, c_v.at[0:7])
    remote(4, "leaf", c_r.at[core], c_r.at[core], sibling).start()

    h_v[...] = (po_v[...] + mmt(xs_v[...], c_r[core].reshape(R, R))).astype(BF16).reshape(D, 2 * C, R)
    for j in grp_peers:
        remote(6, "grp", h_v.at[j], h_r.at[g], j).start()
    h_r[g] = h_v[g]

    arrived(4, c_v)
    im_v[...] = (loc_v[...] + mmt(vr_v[...], c_r[...].reshape(K, R))).astype(BF16)
    for t in range(3):
        rows = pl.ds(t * 512, 512)
        img_v[rows, :] = mm(pt_v[rows, :], im_v[...]).astype(BF16)

    arrived(6, h_r.at[0:15])
    total = h_r[0].astype(F32)
    for j in range(1, D):
        total = total + h_r[j].astype(F32)
    z_v[...] = total.astype(BF16)
    for j in z_peers:
        remote(7, "leaf", z_v, z_r.at[z], j).start()
    z_r[z] = z_v[...]
    arrived(7, z_r.at[0:7])
    total = z_r[0].astype(F32)
    for j in range(1, D // 2):
        total = total + z_r[j].astype(F32)
    f_v[...] = total.astype(BF16)
    for j in grp_peers:
        remote(8, "grp", f_v, f_r.at[g], j).start()
        pltpu.make_async_remote_copy(
            src_ref=f_v, dst_ref=o_r.at[g], send_sem=send_sem.at[9], recv_sem=recv_sem.at[9],
            device_id={"grp": j, "leaf": sibling}, device_id_type=pl.DeviceIdType.MESH).start()
    remote(9, "leaf", f_v, o_r.at[g], sibling).start()
    f_r[g] = f_v[...]
    arrived(8, f_r.at[0:15])
    scale = 1.0 / (N * D * D)
    out_v[:, :, own_half] = (f_r[...].astype(F32) * scale).reshape(2, K, R)
    arrived(9, o_r)
    out_v[:, :, other_half] = (o_r[...].astype(F32) * scale).reshape(2, K, R)
    for phase, ref in enumerate((
        l1_v.at[0:15], s0_v, b_r.at[0:15], c_v.at[0:7], c_v, ps_v, h_v.at[0:15], z_r.at[0:7], f_r.at[0:15], f_r, xv_v,
    )):
        left(phase, ref)


def finish(image, grams, img_h, cur_h, cor_h, sem):
    rows = [pl.ds(t * 256, 256) for t in range(N // 256)]
    pairs = [(image.at[r], img_h.at[r]) for r in rows]
    pairs += [(grams.at[i, pl.ds(t * 128, 128)], dst.at[pl.ds(t * 128, 128)]) for i, dst in enumerate((cur_h, cor_h)) for t in range(2)]
    copies = [pltpu.make_async_copy(src, dst, sem.at[i]) for i, (src, dst) in enumerate(pairs)]
    for copy in copies:
        copy.start()
    for copy in copies:
        copy.wait()


def body(*args):
    any_spec = pl.BlockSpec(memory_space=pl.ANY)
    vmem_spec = pl.BlockSpec(memory_space=pltpu.VMEM)
    dma = pltpu.SemaphoreType.DMA
    v = pltpu.VMEM
    scratch = [
        v((N, K), BF16), v((N, K), BF16), v((1, N), jnp.int32), v((N, N), BF16), v((N, R), BF16), v((N, R), BF16),
        v((3, R, R), BF16), v((3, 14, R, R), BF16), v((28, R, R), BF16), v((7, R, R), BF16),
        v((N, N), BF16), v((N, N), BF16), v((N, K), BF16), v((2 * K, N), BF16), v((N, K), F32), v((N, K), BF16),
        v((K, R), BF16), v((K, R), BF16), v((D, C, R), BF16), v((D, C, R), BF16), v((C, R), BF16), v((D, C, R), BF16),
        v((D, R, R), BF16), v((8 * R, R), BF16), v((8 * R, R), BF16), v((N, R), BF16), v((2 * K, R), BF16), v((8, C, R), BF16), v((2, 8, C, R), BF16),
        v((2 * K, K), F32), v((2 * K, R), BF16), v((2 * K, R), BF16), v((2 * K, R), F32), v((2 * K, R), BF16), v((2 * K, R), BF16),
        v((D, 2 * C, R), BF16), v((D, 2 * C, R), BF16), v((2 * C, R), BF16), v((8, 2 * C, R), BF16), v((2 * C, R), BF16),
        v((D, 2 * C, R), BF16), v((D, 2 * C, R), BF16),
        dma((10,)), dma((11,)), dma((11,)),
    ]
    args = [pltpu.with_memory_space_constraint(a, pltpu.HBM) for a in args[:-1]] + [args[-1]]
    image, grams = pl.pallas_call(
        kernel,
        out_shape=(jax.ShapeDtypeStruct((N, K), BF16), jax.ShapeDtypeStruct((2, K, K), F32)),
        in_specs=[any_spec] * 9 + [pl.BlockSpec(memory_space=pltpu.SMEM)],
        out_specs=(vmem_spec, vmem_spec),
        scratch_shapes=scratch,
        compiler_params=pltpu.CompilerParams(
            collective_id=0, has_side_effects=True, vmem_limit_bytes=48 * 1024 * 1024),
    )(*args)
    return pl.pallas_call(
        finish,
        out_shape=(jax.ShapeDtypeStruct((N, K), BF16), jax.ShapeDtypeStruct((K, K), F32), jax.ShapeDtypeStruct((K, K), F32)),
        in_specs=[any_spec, any_spec],
        out_specs=(any_spec, any_spec, any_spec),
        scratch_shapes=[dma((10,))],
        compiler_params=pltpu.CompilerParams(vmem_limit_bytes=1024 * 1024),
    )(image, grams)


def solution(mesh):
    in_specs = (
        P(GRP_LEAF, None), P(GRP_LEAF, None), P(GRP_LEAF, None), P(GRP_LEAF, None, None), P(GRP_LEAF, None, None),
        P(GRP_LEAF, None, None), P(None, GRP_LEAF, None, None), P(None, "grp", None, None), P(), P(),
    )
    return jax.shard_map(
        body, mesh=mesh, in_specs=in_specs, out_specs=(P(GRP_LEAF, None), P(), P()), check_vma=False)
```
